128 devices in a mesh: file: 4 (over z), rows: 32 (over x, y, core).
Axes of the slice: x: 4, y: 4, z: 4, core: 2. Of those that a mesh axis runs over, the one named last changes fastest.
Arguments:
- snapshots: float32 [16384, 2048], P('rows', 'file'), may hold values from -4000 to 4000
- part_map: int32 [16384], replicated, may hold values from 0 to 16383, as said below
- jac_blocks: float32 [16384, 8, 4096], P(('file', 'rows')), may hold values from -2 to 8
- jac_cols: int32 [16384, 8], P(('file', 'rows')), may hold values from -1 to 16383, as said below
Outputs:
- basis: float32 [16384, 2048], P(('file', 'rows'))
- jac_basis: float32 [16384, 2048], P(('file', 'rows'))
- reduced: float32 [32, 32], replicated
The draws below stay inside these ranges and needn't reach their ends.
Inputs may be any that keep to these rules, and one draw needn't show every extreme that they name: `part_map`: A permutation of the cell blocks. The 128 slots of each partition hold exactly 1 block of each group of 128 consecutive cell blocks, in no particular order. `jac_cols`: in each row, entry 0 is the row's own slot s, the valid entries come first and -1 pads the rest; each row has 3 to 8 valid entries and some row has 8. Every valid entry lies in the partition of s, in the last 32 slots of the partition before it, or in the first 32 slots of the partition after it.
All inputs are finite; a program needn't handle non-finite values.
Results may differ from the reference program's by a relative error of at most 0.0001.
Values sent between devices are 32-bit elements; how exact they have to be, the bound alone decides.
No kernel may reach another device: no remote copies, remote signals or barrier semaphores. Data moves between devices by JAX's collectives and lax.ppermute only.
A program may use at most 192 MiB of HBM per device.

```python
import math
import jax
import jax.numpy as jnp
from jax import lax

NSNAP = 32
BS = 64
NNZB = 8
RIM = 32
BPD = 128
NPART = 128
BPC = 1
NBLK = 16384
NROWS = 1048576


def layout_map(key):
    base = jax.random.fold_in(key, 3)
    group_keys = jax.random.split(base, NPART)
    orders = jax.vmap(lambda subkey: jax.random.permutation(subkey, BPD))(group_keys)
    owned = orders + (jnp.arange(NPART) * BPD)[:, None]
    owned = owned.reshape(NPART, NPART, BPC).transpose(1, 0, 2).reshape(NPART, BPD)
    shuffle_keys = jax.random.split(jax.random.fold_in(base, 1), NPART)
    shuffles = jax.vmap(lambda subkey: jax.random.permutation(subkey, BPD))(shuffle_keys)
    return jnp.take_along_axis(owned, shuffles, axis=1).reshape(NBLK).astype(jnp.int32)


def draw_part_map(key, part):
    return layout_map(key)


def draw_jac_cols(key, part):
    base = jax.random.fold_in(key, 17)
    key_own, key_rim, key_count = jax.random.split(base, 3)
    slots = jnp.arange(NBLK, dtype=jnp.int32)
    owner = slots // BPD
    within = slots % BPD
    own = owner[:, None] * BPD + jax.random.randint(key_own, (NBLK, NNZB), 0, BPD)
    rim_pick = jax.random.randint(key_rim, (NBLK,), 0, RIM)
    left_ok = (within < RIM) & (owner > 0)
    right_ok = (within >= BPD - RIM) & (owner < NPART - 1)
    left = (owner - 1) * BPD + BPD - RIM + rim_pick
    right = (owner + 1) * BPD + rim_pick
    cross = jnp.where(left_ok, left, jnp.where(right_ok, right, own[:, 1]))
    columns = own.at[:, 0].set(slots).at[:, 1].set(cross)
    count = jax.random.randint(key_count, (NBLK,), 3, NNZB + 1)
    count = jnp.where(within == 0, NNZB, count)
    keep = jnp.arange(NNZB)[None, :] < count[:, None]
    return jnp.where(keep, columns, -1).astype(jnp.int32)


def draw_snapshots(key, part):
    regions = 16
    cell_rows = (jnp.arange(NBLK)[:, None] * BS + jnp.arange(BS)[None, :]).astype(jnp.float32)
    region = jnp.arange(NBLK) * regions // NBLK
    col_scale = jnp.exp(jax.random.uniform(jax.random.fold_in(key, 5), (regions, NSNAP), jnp.float32, 0.0, math.log(10.0)))
    rough = jnp.exp(jax.random.uniform(jax.random.fold_in(key, 19), (NBLK, BS), jnp.float32, 0.0, math.log(10.0)))
    ramp = 1.0 + 2.0 * cell_rows / float(NROWS - 1)
    values = jnp.clip(jax.random.normal(jax.random.fold_in(key, 23), (NBLK, NSNAP, BS), jnp.float32), -6.0, 6.0)
    values = values * col_scale[region][:, :, None] * (rough * ramp)[:, None, :]
    return values.reshape(NBLK, NSNAP * BS)


def draw_jac_blocks(key, part):
    regions = 16
    slot_map = layout_map(key)
    region_of = slot_map * regions // NBLK
    factor = jnp.exp(jax.random.uniform(jax.random.fold_in(key, 7), (regions,), jnp.float32, 0.0, math.log(4.0)))
    diag_vals = factor[region_of][:, None] * jax.random.uniform(jax.random.fold_in(key, 31), (NBLK, BS), jnp.float32, 0.5, 1.5)
    noise = jnp.clip(jax.random.normal(jax.random.fold_in(key, 37), (NBLK, NNZB, BS * BS), jnp.float32), -6.0, 6.0)
    noise = noise * float(BS) ** (-0.5)
    identity = (jnp.arange(BS)[:, None] == jnp.arange(BS)[None, :]).astype(jnp.float32)
    diagonal = (diag_vals[:, :, None] * identity[None, :, :]).reshape(NBLK, BS * BS)
    self_mask = (jnp.arange(NNZB) == 0).astype(jnp.float32)
    return noise + self_mask[None, :, None] * diagonal[:, None, :]


def setup_inputs(seed: int = 0) -> dict:
    keys = jax.random.split(jax.random.key(seed), 5)
    snapshots = draw_snapshots(jax.random.fold_in(keys[4], 71), 0)
    part_map = draw_part_map(jax.random.fold_in(keys[4], 71), 0)
    jac_blocks = draw_jac_blocks(jax.random.fold_in(keys[4], 71), 0)
    jac_cols = draw_jac_cols(jax.random.fold_in(keys[4], 71), 0)
    return {"snapshots": snapshots, "part_map": part_map, "jac_blocks": jac_blocks, "jac_cols": jac_cols}


def reference(snapshots, part_map, jac_blocks, jac_cols):
    high = lax.Precision.HIGHEST
    blocks = snapshots.shape[0]
    snap_three = snapshots.reshape(blocks, NSNAP, BS)
    gram = jnp.einsum('bjc,bkc->jk', snap_three, snap_three, precision=high)
    lower = jnp.linalg.cholesky(gram)
    identity = jnp.eye(NSNAP, dtype=jnp.float32)
    inverse = jax.scipy.linalg.solve_triangular(lower, identity, lower=True)
    scaled = inverse * float(NROWS) ** 0.5
    modes = jnp.einsum('kj,bjc->bkc', scaled, snap_three, precision=high)
    basis = jnp.take(modes, part_map.astype(jnp.int32), axis=0)
    total = jnp.zeros_like(basis)
    for entry in range(NNZB):
        column = jac_cols[:, entry]
        valid = column >= 0
        picked = jnp.take(basis, jnp.maximum(column, 0).astype(jnp.int32), axis=0)
        block = jac_blocks[:, entry].reshape(blocks, BS, BS)
        term = jnp.einsum('bkc,brc->bkr', picked, block, precision=high)
        total = total + jnp.where(valid[:, None, None], term, jnp.float32(0.0))
    reduced = jnp.einsum('bkc,blc->kl', basis, total, precision=high) / float(NROWS)
    return (basis.reshape(blocks, NSNAP * BS), total.reshape(blocks, NSNAP * BS), reduced)
```

```python
import jax
import jax.numpy as jnp
from jax import lax
from jax.experimental import pallas as pl
from jax.experimental.pallas import tpu as pltpu
from jax.sharding import PartitionSpec as P

NSNAP = 32
BS = 64
NNZB = 8
RIM = 32
HALF = NSNAP // 2
LANES = 128
AXES = ("file", "rows")
VMEM = pltpu.VMEM
SMEM = pltpu.SMEM
NT = (((1,), (1,)), ((), ()))
HIGH = lax.Precision.HIGHEST


def spec(space):
    return pl.BlockSpec(memory_space=space)


def limit(mib):
    return pltpu.CompilerParams(vmem_limit_bytes=mib * 1024 * 1024)


def cost(flops, nbytes):
    return pl.CostEstimate(flops=flops, bytes_accessed=nbytes, transcendentals=0)


def low_half(shape):
    return lax.broadcasted_iota(jnp.int32, shape, len(shape) - 1) < BS


def split_pair(first, second):
    low = low_half(first.shape)
    zero = jnp.where(low, first, pltpu.roll(second, BS, 1))
    one = jnp.where(low, pltpu.roll(first, BS, 1), second)
    return zero, one


def pack_kernel(rows_ref, snap_ref, out_ref):
    per_pair = out_ref.shape[1] // 4

    def body(part, carry):
        for q in range(per_pair):
            row = rows_ref[part * per_pair + q]
            out_ref[part, 4 * q : 4 * q + 4, :] = snap_ref[pl.ds(row, 4, stride=8), :]
        return carry

    lax.fori_loop(0, out_ref.shape[0], body, 0, unroll=4)


def pack(snapshots, rows, n_part):
    blocks, width = snapshots.shape
    tiles = width // LANES
    view = snapshots.reshape(blocks // 8, 8, tiles, LANES).transpose(0, 2, 1, 3)
    view = view.reshape(blocks * tiles, LANES)
    per_pair = blocks // n_part
    return pl.pallas_call(
        pack_kernel,
        out_shape=jax.ShapeDtypeStruct((n_part, per_pair * tiles, LANES), jnp.float32),
        in_specs=[spec(SMEM), spec(VMEM)],
        out_specs=spec(VMEM),
        name="pack",
    )(rows, view)


def split_kernel(jac_ref, high_ref, low_ref):
    def body(s, carry):
        for pair in range(NNZB // 2):
            for tb in range(2):
                first = jac_ref[s, pl.ds(tb * 128 + 2 * pair, 16, stride=8), :]
                second = jac_ref[s, pl.ds(tb * 128 + 2 * pair + 1, 16, stride=8), :]
                for r2, part in enumerate(split_pair(first, second)):
                    high = part.astype(jnp.bfloat16)
                    low = (part - high.astype(jnp.float32)).astype(jnp.bfloat16)
                    where = (s, slice(32 * r2 + 16 * tb, 32 * r2 + 16 * tb + 16), slice(128 * pair, 128 * pair + 128))
                    high_ref[where] = high
                    low_ref[where] = low
        return carry

    lax.fori_loop(0, jac_ref.shape[0], body, 0)


def split_blocks(jac_blocks):
    slots = jac_blocks.shape[0]
    view = jac_blocks.reshape(slots, NNZB, BS * BS // LANES, LANES).transpose(0, 2, 1, 3)
    view = view.reshape(slots, NNZB * BS * BS // LANES, LANES)
    step = 8
    out = jax.ShapeDtypeStruct((slots, BS, NNZB * BS), jnp.bfloat16)
    return pl.pallas_call(
        split_kernel,
        out_shape=(out, out),
        grid=(slots // step,),
        in_specs=[pl.BlockSpec((step,) + view.shape[1:], lambda i: (i, 0, 0))],
        out_specs=[pl.BlockSpec((step,) + out.shape[1:], lambda i: (i, 0, 0))] * 2,
        cost_estimate=cost(0, 32 * 1024 * 1024),
        name="split_blocks",
    )(view)


def assemble_kernel(rows_ref, recv_ref, snap_ref, pairs_ref, gram_ref):
    slots = snap_ref.shape[0]
    per_file = recv_ref.shape[0] // 4

    def body(s, carry):
        row = rows_ref[s]
        for f in range(4):
            snap_ref[s, 4 * f : 4 * f + 4, :] = recv_ref[pl.ds(f * per_file + row, 4), :]
        return carry

    lax.fori_loop(0, slots, body, 0, unroll=4)
    for sp in range(slots // 2):
        zero, one = split_pair(snap_ref[2 * sp], snap_ref[2 * sp + 1])
        pairs_ref[0:HALF, sp * LANES : sp * LANES + LANES] = zero
        pairs_ref[HALF:NSNAP, sp * LANES : sp * LANES + LANES] = one
    pairs = pairs_ref[...]
    gram_ref[...] = lax.dot_general(pairs, pairs, NT, precision=HIGH, preferred_element_type=jnp.float32)


def assemble(received, rows, slots):
    return pl.pallas_call(
        assemble_kernel,
        out_shape=(
            jax.ShapeDtypeStruct((slots, HALF, LANES), jnp.float32),
            jax.ShapeDtypeStruct((NSNAP, slots * BS), jnp.float32),
            jax.ShapeDtypeStruct((NSNAP, NSNAP), jnp.float32),
        ),
        in_specs=[spec(SMEM), spec(VMEM)],
        out_specs=(spec(VMEM),) * 3,
        name="assemble",
    )(rows, received.reshape(-1, LANES))


def apply_kernel(cols_ref, lo_ref, own_ref, hi_ref, pairs_ref, jh_ref, jl_ref, out_ref, red_ref, xh_ref, xl_ref):
    g = pl.program_id(0)
    low16 = low_half((HALF, LANES))

    @pl.when(g == 0)
    def _():
        def fill(ref, base, count):
            def body(s, carry):
                x = ref[s]
                y = pltpu.roll(x, BS, 1)
                for kk, part in enumerate((jnp.where(low16, x, y), jnp.where(low16, y, x))):
                    high = part.astype(jnp.bfloat16)
                    low = (part - high.astype(jnp.float32)).astype(jnp.bfloat16)
                    xh_ref[base + s, HALF * kk : HALF * kk + HALF, :] = high
                    xl_ref[base + s, HALF * kk : HALF * kk + HALF, :] = low
                return carry

            lax.fori_loop(0, count, body, 0, unroll=2)

        slots = own_ref.shape[0]
        fill(lo_ref, 0, RIM)
        fill(own_ref, RIM, slots)
        fill(hi_ref, RIM + slots, RIM)
        xh_ref[slots + 2 * RIM] = jnp.zeros((NSNAP, LANES), jnp.bfloat16)
        xl_ref[slots + 2 * RIM] = jnp.zeros((NSNAP, LANES), jnp.bfloat16)
        red_ref[...] = jnp.zeros_like(red_ref)

    low32 = low_half((NSNAP, LANES))
    lane = lax.broadcasted_iota(jnp.int32, (NSNAP, LANES), 1)
    r = lane % BS
    order = lane - r + (r % 2) * (BS // 2) + r // 2
    group = 4
    for sub in range(jh_ref.shape[0] // group):
        highs, lows = [], []
        for i in range(group):
            hi_parts, lo_parts = [], []
            for pair in range(NNZB // 2):
                at = ((g * (jh_ref.shape[0]) + sub * group + i) * NNZB) + 2 * pair
                a = cols_ref[at]
                b = cols_ref[at + 1]
                hi_parts.append(jnp.where(low32, xh_ref[a], xh_ref[b]))
                lo_parts.append(jnp.where(low32, xl_ref[a], xl_ref[b]))
            highs.append(jnp.concatenate(hi_parts, axis=1))
            lows.append(jnp.concatenate(lo_parts, axis=1))
        high = jnp.concatenate(highs, axis=0)
        both = jnp.concatenate(highs + lows, axis=0)
        jh = jh_ref[sub * group : sub * group + group].reshape(group * BS, NNZB * BS)
        jl = jl_ref[sub * group : sub * group + group].reshape(group * BS, NNZB * BS)
        big = lax.dot_general(both, jh, NT, preferred_element_type=jnp.float32)
        acc = big[0 : group * NSNAP] + big[group * NSNAP :]
        acc = acc + lax.dot_general(high, jl, NT, preferred_element_type=jnp.float32)
        outs = []
        for ip in range(group // 2):
            tile = acc[:, LANES * ip : LANES * ip + LANES]
            top = tile[2 * ip * NSNAP : 2 * ip * NSNAP + NSNAP]
            bottom = tile[2 * ip * NSNAP + NSNAP : 2 * ip * NSNAP + 2 * NSNAP]
            mixed = jnp.where(low32, top, bottom)
            mixed = jnp.take_along_axis(mixed, order, axis=1)
            outs.append(mixed)
            first, second = split_pair(mixed[0:HALF], mixed[HALF:NSNAP])
            out_ref[sub * group + 2 * ip] = first
            out_ref[sub * group + 2 * ip + 1] = second
        width = group // 2 * LANES
        red_ref[...] += lax.dot_general(
            pairs_ref[:, sub * width : sub * width + width],
            jnp.concatenate(outs, axis=1),
            NT,
            precision=HIGH,
            preferred_element_type=jnp.float32,
        )


def apply_blocks(cols, lo, own, hi, pairs, jac_high, jac_low):
    slots = own.shape[0]
    step = 8
    block = (step, BS, NNZB * BS)
    whole = lambda shape: pl.BlockSpec(shape, lambda i: (0,) * len(shape))
    return pl.pallas_call(
        apply_kernel,
        out_shape=(
            jax.ShapeDtypeStruct((slots, HALF, LANES), jnp.float32),
            jax.ShapeDtypeStruct((NSNAP, NSNAP), jnp.float32),
        ),
        grid=(slots // step,),
        in_specs=[
            spec(SMEM),
            whole(lo.shape),
            whole(own.shape),
            whole(hi.shape),
            pl.BlockSpec((NSNAP, step * BS), lambda i: (0, i)),
            pl.BlockSpec(block, lambda i: (i, 0, 0)),
            pl.BlockSpec(block, lambda i: (i, 0, 0)),
        ],
        out_specs=(
            pl.BlockSpec((step, HALF, LANES), lambda i: (i, 0, 0)),
            whole((NSNAP, NSNAP)),
        ),
        scratch_shapes=[
            pltpu.VMEM((slots + 2 * RIM + 1, NSNAP, LANES), jnp.bfloat16),
            pltpu.VMEM((slots + 2 * RIM + 1, NSNAP, LANES), jnp.bfloat16),
        ],
        compiler_params=limit(32),
        cost_estimate=cost(2 * 3 * slots * 4 * NSNAP * 512 * BS, 24 * 1024 * 1024),
        name="apply_blocks",
    )(cols, lo, own, hi, pairs, jac_high, jac_low)


def factor_kernel(total_rows, gram_ref, scaled_ref):
    row = lax.broadcasted_iota(jnp.int32, (NSNAP, LANES), 0)
    lane = lax.broadcasted_iota(jnp.int32, (NSNAP, LANES), 1)
    rank = 2 * (row % HALF) + row // HALF
    unit = jnp.where(lane - NSNAP == row, 1.0, 0.0).astype(jnp.float32)
    work = jnp.concatenate([gram_ref[...], jnp.zeros((NSNAP, LANES - NSNAP), jnp.float32)], axis=1) + unit
    for k in range(NSNAP):
        at = (k % 2) * HALF + k // 2
        pivot_row = jnp.broadcast_to(work[at : at + 1, :], (NSNAP, LANES))
        pivot_col = jnp.broadcast_to(work[:, at : at + 1], (NSNAP, LANES))
        pivot = jnp.broadcast_to(work[at : at + 1, at : at + 1], (NSNAP, LANES))
        ratio = jnp.where(rank > k, pivot_col / pivot, 0.0)
        work = work - ratio * pivot_row
    diag = jnp.sum(jnp.where(lane == row, work, 0.0), axis=1, keepdims=True)
    scale = float(total_rows) ** 0.5 / jnp.sqrt(diag)
    scaled_ref[...] = (pltpu.roll(work, LANES - NSNAP, 1) * scale)[:, 0:NSNAP]


def factor(gram, total_rows):
    return pl.pallas_call(
        lambda *refs: factor_kernel(total_rows, *refs),
        out_shape=jax.ShapeDtypeStruct((NSNAP, NSNAP), jnp.float32),
        in_specs=[spec(VMEM)],
        out_specs=spec(VMEM),
        cost_estimate=cost(32 * 32 * 128 * 4, 8192),
        name="factor",
    )(gram)


def mix_kernel(scaled_ref, snap_ref, jac_ref, basis_ref, out_ref, same_ref, swap_ref):
    low = low_half((HALF, LANES))

    @pl.when(pl.program_id(0) == 0)
    def _():
        scaled = scaled_ref[...]
        wide = lambda rows, j: jnp.broadcast_to(scaled[rows * HALF : rows * HALF + HALF, j : j + 1], (HALF, LANES))
        for j2 in range(HALF):
            same_ref[j2] = jnp.where(low, wide(0, j2), wide(1, HALF + j2))
            swap_ref[j2] = jnp.where(low, wide(0, HALF + j2), wide(1, j2))

    for source, target in ((snap_ref, basis_ref), (jac_ref, out_ref)):
        for s8 in range(target.shape[0] // 8):
            plain = [source[pl.ds(s8 * 8 * HALF + j2, 8, stride=HALF), :] for j2 in range(HALF)]
            turned = [pltpu.roll(x, BS, 1) for x in plain]
            for k2 in range(HALF):
                total = None
                for j2 in range(k2 + 1):
                    for coef, value in ((same_ref, plain[j2]), (swap_ref, turned[j2])):
                        term = jnp.broadcast_to(coef[j2, k2 : k2 + 1, :], (8, LANES)) * value
                        total = term if total is None else total + term
                target[8 * s8 : 8 * s8 + 8, LANES * k2 : LANES * k2 + LANES] = total


def mix(scaled, snaps, jac):
    slots = snaps.shape[0]
    step = 16
    out = jax.ShapeDtypeStruct((slots, NSNAP * BS), jnp.float32)
    flat = lambda x: x.reshape(slots * HALF, LANES)
    return pl.pallas_call(
        mix_kernel,
        out_shape=(out, out),
        grid=(slots // step,),
        in_specs=[
            pl.BlockSpec((NSNAP, NSNAP), lambda i: (0, 0)),
            pl.BlockSpec((step * HALF, LANES), lambda i: (i, 0)),
            pl.BlockSpec((step * HALF, LANES), lambda i: (i, 0)),
        ],
        out_specs=[pl.BlockSpec((step, NSNAP * BS), lambda i: (i, 0))] * 2,
        scratch_shapes=[pltpu.VMEM((HALF, HALF, LANES), jnp.float32)] * 2,
        cost_estimate=cost(2 * 2 * slots * BS * NSNAP * NSNAP, 4 * 1024 * 1024),
        name="mix",
    )(scaled, flat(snaps), flat(jac))


def finish_kernel(total_rows, scaled_ref, red_ref, out_ref):
    row = lax.broadcasted_iota(jnp.int32, (NSNAP, NSNAP), 0)
    col = lax.broadcasted_iota(jnp.int32, (NSNAP, NSNAP), 1)
    place = jnp.where(col == (row % 2) * HALF + row // 2, 1.0, 0.0).astype(jnp.float32)
    dot = lambda a, b, dims: lax.dot_general(a, b, dims, precision=HIGH, preferred_element_type=jnp.float32)
    nn = (((1,), (0,)), ((), ()))
    natural = dot(place, scaled_ref[...], nn)
    out_ref[...] = dot(dot(natural, red_ref[...], nn), natural, NT) / float(total_rows)


def finish(scaled, reduced, total_rows):
    return pl.pallas_call(
        lambda *refs: finish_kernel(total_rows, *refs),
        out_shape=jax.ShapeDtypeStruct((NSNAP, NSNAP), jnp.float32),
        in_specs=[spec(VMEM)] * 2,
        out_specs=spec(VMEM),
        name="finish",
    )(scaled, reduced)


def total_over_devices(block, n_part):
    copies = jnp.broadcast_to(block.reshape(1, 8, LANES), (n_part, 8, LANES))
    copies = lax.all_to_all(copies, AXES, split_axis=0, concat_axis=0, tiled=True)
    return jnp.sum(copies, axis=0).reshape(NSNAP, NSNAP)


def shards(snapshots, part_map, jac_blocks, jac_cols):
    n_file = lax.axis_size("file")
    n_rows = lax.axis_size("rows")
    n_part = n_file * n_rows
    file_pos = lax.axis_index("file")
    rows_pos = lax.axis_index("rows")
    blocks = jac_blocks.shape[0]
    held = snapshots.shape[0]
    per_pair = held // blocks
    total_rows = blocks * BS * n_part
    my_part = file_pos * n_rows + rows_pos

    local = part_map.reshape(n_part, blocks) - rows_pos * held
    group = jnp.arange(per_pair, dtype=jnp.int32)
    taken = jnp.sum(jnp.where((local >> 7)[:, None, :] == group[None, :, None], local[:, None, :], 0), axis=2)
    send_rows = ((taken >> 3) * 32 + (taken & 7)).reshape(n_part * per_pair)
    packed = pack(snapshots, send_rows, n_part)
    received = lax.all_to_all(packed, AXES, split_axis=0, concat_axis=0, tiled=True)

    jac_high, jac_low = split_blocks(jac_blocks)
    received, jac_high, jac_low = lax.optimization_barrier((received, jac_high, jac_low))

    my_slots = lax.dynamic_slice_in_dim(part_map, my_part * blocks, blocks)
    recv_rows = (my_slots // held) * (4 * per_pair) + ((my_slots >> 7) % per_pair) * 4
    snaps, pairs, part_gram = assemble(received, recv_rows, blocks)

    forward = [(i, i + 1) for i in range(n_part - 1)]
    backward = [(b, a) for a, b in forward]
    lo = lax.ppermute(snaps[blocks - RIM :], AXES, forward)
    hi = lax.ppermute(snaps[:RIM], AXES, backward)
    gram = total_over_devices(part_gram, n_part)

    extended = blocks + 2 * RIM
    where = jnp.clip(jac_cols - (my_part * blocks - RIM), 0, extended - 1)
    cols = jnp.where(jac_cols >= 0, where, extended).reshape(blocks * NNZB)
    jac_snaps, part_reduced = apply_blocks(cols, lo, snaps, hi, pairs, jac_high, jac_low)

    reduced = total_over_devices(part_reduced, n_part)
    scaled = factor(gram, total_rows)
    basis, jac_basis = mix(scaled, snaps, jac_snaps)
    return basis, jac_basis, finish(scaled, reduced, total_rows)


def solution(mesh):
    in_specs = (P("rows", "file"), P(), P(AXES, None, None), P(AXES, None))
    out_specs = (P(AXES, None), P(AXES, None), P())
    return jax.shard_map(shards, mesh=mesh, in_specs=in_specs, out_specs=out_specs, check_vma=False)
```

```python
import jax
import jax.numpy as jnp
from jax import lax
from jax.experimental import pallas as pl
from jax.experimental.pallas import tpu as pltpu
from jax.sharding import PartitionSpec as P

NSNAP = 32
BS = 64
NNZB = 8
RIM = 32
HALF = NSNAP // 2
LANES = 128
AXES = ("file", "rows")
VMEM = pltpu.VMEM
SMEM = pltpu.SMEM
NT = (((1,), (1,)), ((), ()))
HIGH = lax.Precision.HIGHEST


def spec(space):
    return pl.BlockSpec(memory_space=space)


def limit(mib):
    return pltpu.CompilerParams(vmem_limit_bytes=mib * 1024 * 1024)


def cost(flops, nbytes):
    return pl.CostEstimate(flops=flops, bytes_accessed=nbytes, transcendentals=0)


def low_half(shape):
    return lax.broadcasted_iota(jnp.int32, shape, len(shape) - 1) < BS


def split_pair(first, second):
    low = low_half(first.shape)
    zero = jnp.where(low, first, pltpu.roll(second, BS, 1))
    one = jnp.where(low, pltpu.roll(first, BS, 1), second)
    return zero, one


def send_copies(block, out_ref):
    tile = jnp.concatenate([block[8 * i : 8 * i + 8, 0:NSNAP] for i in range(4)], axis=1)
    for p in range(out_ref.shape[0]):
        out_ref[p] = tile


def sum_copies(ref):
    parts = [ref[p] for p in range(ref.shape[0])]
    while len(parts) > 1:
        parts = [x + y for x, y in zip(parts[0::2], parts[1::2])]
    tile = parts[0]
    return jnp.concatenate([tile] + [pltpu.roll(tile, LANES - NSNAP * i, 1) for i in range(1, 4)], axis=0)


def my_part():
    return lax.axis_index("file") * lax.axis_size("rows") + lax.axis_index("rows")


def pack_kernel(map_ref, snap_hbm, out_ref, recv_ref, snap_ref, index_ref, rows_ref, snap_sem, rows_sem):
    fetch = pltpu.make_async_copy(snap_hbm, snap_ref, snap_sem)
    fetch.start()
    n_part, slots = map_ref.shape
    per_pair = out_ref.shape[1] // 4
    held = slots * per_pair

    local = map_ref[...] - lax.axis_index("rows") * held
    group = local >> 7
    within = (local & 127).astype(jnp.float32)
    ones = jnp.ones((8, slots), jnp.bfloat16)
    for q in range(per_pair):
        part = jnp.where(group == q, within, 0.0).astype(jnp.bfloat16)
        found = lax.dot_general(ones, part, NT, preferred_element_type=jnp.float32)
        row = found[0:1].astype(jnp.int32) + q * slots
        index_ref[q : q + 1, :] = (row >> 3) * 32 + (row & 7)
    move = pltpu.make_async_copy(index_ref, rows_ref, rows_sem)
    move.start()

    mine = map_ref[pl.ds(my_part(), 1), :]
    recv_ref[...] = (mine >> 9) * (4 * per_pair) + ((mine >> 7) & (per_pair - 1)) * 4
    move.wait()
    fetch.wait()

    def body(part, carry):
        for q in range(per_pair):
            row = rows_ref[q, part]
            out_ref[part, 4 * q : 4 * q + 4, :] = snap_ref[pl.ds(row, 4, stride=8), :]
        return carry

    lax.fori_loop(0, n_part, body, 0, unroll=8)


def pack(snapshots, part_map, n_part):
    blocks, width = snapshots.shape
    tiles = width // LANES
    slots = part_map.shape[0] // n_part
    per_pair = blocks // slots
    assert slots == 128 and tiles == 4 and per_pair == 4
    view = snapshots.reshape(blocks // 8, 8, tiles, LANES).transpose(0, 2, 1, 3)
    view = view.reshape(blocks * tiles, LANES)
    return pl.pallas_call(
        pack_kernel,
        out_shape=(
            jax.ShapeDtypeStruct((n_part, per_pair * tiles, LANES), jnp.float32),
            jax.ShapeDtypeStruct((1, slots), jnp.int32),
        ),
        in_specs=[spec(VMEM), spec(pl.ANY)],
        out_specs=(spec(VMEM), spec(VMEM)),
        scratch_shapes=[
            pltpu.VMEM(view.shape, jnp.float32),
            pltpu.VMEM((per_pair, n_part), jnp.int32),
            pltpu.SMEM((per_pair, n_part), jnp.int32),
            pltpu.SemaphoreType.DMA,
            pltpu.SemaphoreType.DMA,
        ],
        compiler_params=limit(60),
        name="pack",
    )(part_map.reshape(n_part, slots), view)


def split_kernel(jac_ref, high_ref, low_ref):
    def body(s, carry):
        for pair in range(NNZB // 2):
            for tb in range(2):
                first = jac_ref[s, pl.ds(tb * 128 + 2 * pair, 16, stride=8), :]
                second = jac_ref[s, pl.ds(tb * 128 + 2 * pair + 1, 16, stride=8), :]
                for r2, part in enumerate(split_pair(first, second)):
                    high = part.astype(jnp.bfloat16)
                    low = (part - high.astype(jnp.float32)).astype(jnp.bfloat16)
                    rows = slice(32 * r2 + 16 * tb, 32 * r2 + 16 * tb + 16)
                    lanes = slice(LANES * pair, LANES * pair + LANES)
                    high_ref[s, rows, lanes] = high
                    low_ref[s, rows, lanes] = low
        return carry

    lax.fori_loop(0, jac_ref.shape[0], body, 0)


def split_blocks(jac_blocks):
    slots = jac_blocks.shape[0]
    view = jac_blocks.reshape(slots, NNZB, BS * BS // LANES, LANES).transpose(0, 2, 1, 3)
    view = view.reshape(slots, NNZB * BS * BS // LANES, LANES)
    step = 16
    out = jax.ShapeDtypeStruct((slots, BS, NNZB * BS), jnp.bfloat16)
    return pl.pallas_call(
        split_kernel,
        out_shape=(out, out),
        grid=(slots // step,),
        in_specs=[pl.BlockSpec((step,) + view.shape[1:], lambda i: (i, 0, 0))],
        out_specs=[pl.BlockSpec((step,) + out.shape[1:], lambda i: (i, 0, 0))] * 2,
        compiler_params=limit(48),
        cost_estimate=cost(0, 32 * 1024 * 1024),
        name="split_blocks",
    )(view)


def assemble_kernel(rows_ref, recv_ref, snap_ref, near_ref, far_ref):
    slots = snap_ref.shape[0]
    per_file = recv_ref.shape[0] // 4

    def body(s, carry):
        row = rows_ref[0, s]
        for f in range(4):
            snap_ref[s, 4 * f : 4 * f + 4, :] = recv_ref[pl.ds(f * per_file + row, 4), :]
        return carry

    lax.fori_loop(0, slots, body, 0, unroll=8)
    odd = my_part() % 2
    near_ref[...] = snap_ref[pl.ds((1 - odd) * (slots - RIM), RIM)]
    far_ref[...] = snap_ref[pl.ds(odd * (slots - RIM), RIM)]


def assemble(received, rows, slots):
    rim = jax.ShapeDtypeStruct((RIM, HALF, LANES), jnp.float32)
    return pl.pallas_call(
        assemble_kernel,
        out_shape=(jax.ShapeDtypeStruct((slots, HALF, LANES), jnp.float32), rim, rim),
        in_specs=[spec(SMEM), spec(VMEM)],
        out_specs=(spec(VMEM),) * 3,
        compiler_params=limit(6),
        name="assemble",
    )(rows, received.reshape(-1, LANES))


def make_pairs(snap_ref, pairs_ref):
    for sp in range(snap_ref.shape[0] // 2):
        zero, one = split_pair(snap_ref[2 * sp], snap_ref[2 * sp + 1])
        pairs_ref[0:HALF, sp * LANES : sp * LANES + LANES] = zero
        pairs_ref[HALF:NSNAP, sp * LANES : sp * LANES + LANES] = one


def gram_kernel(snap_ref, copies_ref, pairs_ref):
    make_pairs(snap_ref, pairs_ref)
    pairs = pairs_ref[...]
    gram = lax.dot_general(pairs, pairs, NT, precision=HIGH, preferred_element_type=jnp.float32)
    send_copies(gram, copies_ref)


def gram_part(snaps, n_part):
    slots = snaps.shape[0]
    return pl.pallas_call(
        gram_kernel,
        out_shape=jax.ShapeDtypeStruct((n_part, 8, LANES), jnp.float32),
        in_specs=[spec(VMEM)],
        out_specs=spec(VMEM),
        scratch_shapes=[pltpu.VMEM((NSNAP, slots * BS), jnp.float32)],
        compiler_params=limit(8),
        cost_estimate=cost(2 * 6 * NSNAP * NSNAP * slots * BS, 3 * 1024 * 1024),
        name="gram_part",
    )(snaps)


CHUNK = 16


def apply_kernel(cols_ref, near_ref, own_ref, far_ref, jh_hbm, jl_hbm, out_ref, copies_ref, xh_ref, xl_ref, pairs_ref, mixed_ref, jh_ref, jl_ref, sems):
    low16 = low_half((HALF, LANES))
    low32 = low_half((NSNAP, LANES))
    slots = own_ref.shape[0]

    def fetch(c):
        rows = pl.ds(c * CHUNK, CHUNK)
        return (
            pltpu.make_async_copy(jh_hbm.at[rows], jh_ref.at[rows], sems.at[0, c]),
            pltpu.make_async_copy(jl_hbm.at[rows], jl_ref.at[rows], sems.at[1, c]),
        )

    for c in range(slots // CHUNK):
        for copy in fetch(c):
            copy.start()

    def fill(ref, base, count):
        def body(s, carry):
            x = ref[s]
            y = pltpu.roll(x, BS, 1)
            for kk, part in enumerate((jnp.where(low16, x, y), jnp.where(low16, y, x))):
                high = part.astype(jnp.bfloat16)
                low = (part - high.astype(jnp.float32)).astype(jnp.bfloat16)
                xh_ref[base + s, HALF * kk : HALF * kk + HALF, :] = high
                xl_ref[base + s, HALF * kk : HALF * kk + HALF, :] = low
            return carry

        lax.fori_loop(0, count, body, 0, unroll=8)

    odd = my_part() % 2
    first_slot = my_part() * slots - RIM
    last_row = slots + 2 * RIM - 1
    fill(near_ref, (1 - odd) * (slots + RIM), RIM)
    fill(own_ref, RIM, slots)
    fill(far_ref, odd * (slots + RIM), RIM)
    xh_ref[last_row + 1] = jnp.zeros((NSNAP, LANES), jnp.bfloat16)
    xl_ref[last_row + 1] = jnp.zeros((NSNAP, LANES), jnp.bfloat16)
    make_pairs(own_ref, pairs_ref)

    def table_row(n, s):
        column = cols_ref[n, s]
        row = jnp.minimum(jnp.maximum(column - first_slot, 0), last_row)
        return jnp.where(column < 0, last_row + 1, row)

    lane = lax.broadcasted_iota(jnp.int32, (NSNAP, LANES), 1)
    r = lane % BS
    order = lane - r + (r % 2) * (BS // 2) + r // 2
    group = 4

    def body(g, carry):
        highs, lows = [], []
        for i in range(group):
            hi_parts, lo_parts = [], []
            for pair in range(NNZB // 2):
                a = table_row(2 * pair, g * group + i)
                b = table_row(2 * pair + 1, g * group + i)
                hi_parts.append(jnp.where(low32, xh_ref[a], xh_ref[b]))
                lo_parts.append(jnp.where(low32, xl_ref[a], xl_ref[b]))
            highs.append(jnp.concatenate(hi_parts, axis=1))
            lows.append(jnp.concatenate(lo_parts, axis=1))
        high = jnp.concatenate(highs, axis=0)
        both = jnp.concatenate(highs + lows, axis=0)
        jh = jh_ref[pl.ds(g * group, group)].reshape(group * BS, NNZB * BS)
        jl = jl_ref[pl.ds(g * group, group)].reshape(group * BS, NNZB * BS)
        big = lax.dot_general(both, jh, NT, preferred_element_type=jnp.float32)
        acc = big[0 : group * NSNAP] + big[group * NSNAP :]
        acc = acc + lax.dot_general(high, jl, NT, preferred_element_type=jnp.float32)
        for ip in range(group // 2):
            tile = acc[:, LANES * ip : LANES * ip + LANES]
            top = tile[2 * ip * NSNAP : 2 * ip * NSNAP + NSNAP]
            bottom = tile[2 * ip * NSNAP + NSNAP : 2 * ip * NSNAP + 2 * NSNAP]
            mixed = jnp.take_along_axis(jnp.where(low32, top, bottom), order, axis=1)
            mixed_ref[:, pl.ds(pl.multiple_of((g * 2 + ip) * LANES, LANES), LANES)] = mixed
            first, second = split_pair(mixed[0:HALF], mixed[HALF:NSNAP])
            out_ref[g * group + 2 * ip] = first
            out_ref[g * group + 2 * ip + 1] = second
        return carry

    def chunk(c, carry):
        for copy in fetch(c):
            copy.wait()
        per_chunk = CHUNK // group
        return lax.fori_loop(c * per_chunk, c * per_chunk + per_chunk, body, carry, unroll=True)

    lax.fori_loop(0, slots // CHUNK, chunk, 0)
    reduced = lax.dot_general(pairs_ref[...], mixed_ref[...], NT, precision=HIGH, preferred_element_type=jnp.float32)
    send_copies(reduced, copies_ref)


def apply_blocks(cols, near, own, far, jac_high, jac_low, n_part):
    slots = own.shape[0]
    table = pltpu.VMEM((slots + 2 * RIM + 1, NSNAP, LANES), jnp.bfloat16)
    wide = pltpu.VMEM((NSNAP, slots * BS), jnp.float32)
    held = pltpu.VMEM(jac_high.shape, jac_high.dtype)
    return pl.pallas_call(
        apply_kernel,
        out_shape=(
            jax.ShapeDtypeStruct((slots, HALF, LANES), jnp.float32),
            jax.ShapeDtypeStruct((n_part, 8, LANES), jnp.float32),
        ),
        in_specs=[spec(SMEM)] + [spec(VMEM)] * 3 + [spec(pl.ANY)] * 2,
        out_specs=(spec(VMEM),) * 2,
        scratch_shapes=[table, table, wide, wide, held, held, pltpu.SemaphoreType.DMA((2, slots // CHUNK))],
        compiler_params=limit(48),
        cost_estimate=cost(2 * 3 * slots * 4 * NSNAP * 512 * BS, 24 * 1024 * 1024),
        name="apply_blocks",
    )(cols, near, own, far, jac_high, jac_low)


def factor(gram, total_rows):
    row = lax.broadcasted_iota(jnp.int32, (NSNAP, LANES), 0)
    lane = lax.broadcasted_iota(jnp.int32, (NSNAP, LANES), 1)
    rank = 2 * (row % HALF) + row // HALF
    unit = jnp.where(lane - NSNAP == row, 1.0, 0.0).astype(jnp.float32)
    work = jnp.where(lane < NSNAP, gram, unit)
    wide = lambda x: jnp.broadcast_to(x, (NSNAP, LANES))
    for k2 in range(HALF):
        p, q = k2, HALF + k2
        row_p, row_q = wide(work[p : p + 1, :]), wide(work[q : q + 1, :])
        col_p, col_q = wide(work[:, p : p + 1]), wide(work[:, q : q + 1])
        a = wide(work[p : p + 1, p : p + 1])
        b = wide(work[q : q + 1, p : p + 1])
        c = wide(work[q : q + 1, q : q + 1])
        ratio = b / a
        row_q = row_q - ratio * row_p
        below = (col_p / a) * row_p + ((col_q - ratio * col_p) / (c - ratio * b)) * row_q
        work = work - jnp.where(rank > 2 * k2 + 1, below, jnp.where(rank == 2 * k2 + 1, ratio * row_p, 0.0))
    diag = jnp.sum(jnp.where(lane == row, work, 0.0), axis=1, keepdims=True)
    scale = float(total_rows) ** 0.5 / jnp.sqrt(diag)
    return pltpu.roll(work, LANES - NSNAP, 1) * scale


def mix_kernel(total_rows, gram_ref, snap_ref, jac_ref, basis_ref, out_ref, scaled_ref, same_ref, swap_ref, plain_ref, turned_ref):
    low = low_half((HALF, LANES))

    @pl.when(pl.program_id(0) == 0)
    def _():
        scaled = factor(sum_copies(gram_ref), total_rows)
        scaled_ref[...] = scaled[:, 0:NSNAP]
        wide = lambda kk, j: jnp.broadcast_to(scaled[kk * HALF : kk * HALF + HALF, j : j + 1], (HALF, LANES))
        for j2 in range(HALF):
            same_ref[j2] = jnp.where(low, wide(0, j2), wide(1, HALF + j2))
            swap_ref[j2] = jnp.where(low, wide(0, HALF + j2), wide(1, j2))

    both = range(2)
    for source, target in ((snap_ref, basis_ref), (jac_ref, out_ref)):
        def body(pair, carry):
            for j2 in range(HALF):
                for h in both:
                    x = source[pl.ds((2 * pair + h) * 8 * HALF + j2, 8, stride=HALF), :]
                    plain_ref[h, j2] = x
                    turned_ref[h, j2] = pltpu.roll(x, BS, 1)
            for k4 in range(0, HALF, 4):
                totals = {}
                for j2 in range(k4 + 4):
                    values = [(plain_ref[h, j2], turned_ref[h, j2]) for h in both]
                    for k2 in range(max(k4, j2), k4 + 4):
                        same = jnp.broadcast_to(same_ref[j2, k2 : k2 + 1, :], (8, LANES))
                        swap = jnp.broadcast_to(swap_ref[j2, k2 : k2 + 1, :], (8, LANES))
                        for h in both:
                            term = same * values[h][0] + swap * values[h][1]
                            totals[k2, h] = totals[k2, h] + term if j2 else term
                for k2 in range(k4, k4 + 4):
                    for h in both:
                        rows = pl.ds(pl.multiple_of((2 * pair + h) * 8, 8), 8)
                        target[rows, LANES * k2 : LANES * k2 + LANES] = totals[k2, h]
            return carry

        lax.fori_loop(0, target.shape[0] // 16, body, 0)


def mix(gram, snaps, jac, total_rows):
    slots = snaps.shape[0]
    step = 32
    out = jax.ShapeDtypeStruct((slots, NSNAP * BS), jnp.float32)
    flat = lambda x: x.reshape(slots * HALF, LANES)
    rows = pl.BlockSpec((step * HALF, LANES), lambda i: (i, 0))
    return pl.pallas_call(
        lambda *refs: mix_kernel(total_rows, *refs),
        out_shape=(out, out, jax.ShapeDtypeStruct((NSNAP, NSNAP), jnp.float32)),
        grid=(slots // step,),
        in_specs=[pl.BlockSpec(gram.shape, lambda i: (0, 0, 0)), rows, rows],
        out_specs=[pl.BlockSpec((step, NSNAP * BS), lambda i: (i, 0))] * 2 + [pl.BlockSpec((NSNAP, NSNAP), lambda i: (0, 0))],
        scratch_shapes=[pltpu.VMEM((HALF, HALF, LANES), jnp.float32)] * 2 + [pltpu.VMEM((2, HALF, 8, LANES), jnp.float32)] * 2,
        cost_estimate=cost(2 * 2 * slots * BS * NSNAP * NSNAP, 4 * 1024 * 1024),
        compiler_params=limit(12),
        name="mix",
    )(gram, flat(snaps), flat(jac))


def finish_kernel(total_rows, scaled_ref, red_ref, out_ref):
    row = lax.broadcasted_iota(jnp.int32, (NSNAP, NSNAP), 0)
    col = lax.broadcasted_iota(jnp.int32, (NSNAP, NSNAP), 1)
    place = jnp.where(col == (row % 2) * HALF + row // 2, 1.0, 0.0).astype(jnp.float32)
    dot = lambda a, b, dims: lax.dot_general(a, b, dims, precision=HIGH, preferred_element_type=jnp.float32)
    nn = (((1,), (0,)), ((), ()))
    natural = dot(place, scaled_ref[...], nn)
    reduced = sum_copies(red_ref)[:, 0:NSNAP]
    out_ref[...] = dot(dot(natural, reduced, nn), natural, NT) / float(total_rows)


def finish(scaled, reduced, total_rows):
    return pl.pallas_call(
        lambda *refs: finish_kernel(total_rows, *refs),
        out_shape=jax.ShapeDtypeStruct((NSNAP, NSNAP), jnp.float32),
        in_specs=[spec(VMEM)] * 2,
        out_specs=spec(VMEM),
        compiler_params=limit(4),
        name="finish",
    )(scaled, reduced)


def exchange(tiles):
    return lax.all_to_all(tiles, AXES, split_axis=0, concat_axis=0, tiled=True)


def shards(snapshots, part_map, jac_blocks, jac_cols):
    n_part = lax.axis_size("file") * lax.axis_size("rows")
    blocks = jac_blocks.shape[0]
    total_rows = blocks * BS * n_part

    packed, recv_rows = pack(snapshots, part_map, n_part)
    received = exchange(packed)
    jac_high, jac_low = split_blocks(jac_blocks)
    received, jac_high, jac_low = lax.optimization_barrier((received, jac_high, jac_low))
    snaps, near, far = assemble(received, recv_rows, blocks)

    near_swap = [(p, p ^ 1) for p in range(n_part)]
    far_swap = [(p, ((p + 1) ^ 1) - 1) for p in range(1, n_part - 1)]
    far = lax.ppermute(far, AXES, far_swap)
    near = lax.ppermute(near, AXES, near_swap)
    gram = exchange(gram_part(snaps, n_part))
    jac_snaps, reduced_tiles = apply_blocks(jac_cols.T, near, snaps, far, jac_high, jac_low, n_part)

    reduced = exchange(reduced_tiles)
    basis, jac_basis, scaled = mix(gram, snaps, jac_snaps, total_rows)
    return basis, jac_basis, finish(scaled, reduced, total_rows)


def solution(mesh):
    in_specs = (P("rows", "file"), P(), P(AXES, None, None), P(AXES, None))
    out_specs = (P(AXES, None), P(AXES, None), P())
    return jax.shard_map(shards, mesh=mesh, in_specs=in_specs, out_specs=out_specs, check_vma=False)
```

```python
import jax
import jax.numpy as jnp
from jax import lax
from jax.experimental import pallas as pl
from jax.experimental.pallas import tpu as pltpu
from jax.sharding import PartitionSpec as P

NSNAP = 32
BS = 64
NNZB = 8
RIM = 32
HALF = NSNAP // 2
LANES = 128
AXES = ("file", "rows")
VMEM = pltpu.VMEM
SMEM = pltpu.SMEM
NT = (((1,), (1,)), ((), ()))
HIGH = lax.Precision.HIGHEST


def spec(space):
    return pl.BlockSpec(memory_space=space)


def limit(mib):
    return pltpu.CompilerParams(vmem_limit_bytes=mib * 1024 * 1024)


def cost(flops, nbytes):
    return pl.CostEstimate(flops=flops, bytes_accessed=nbytes, transcendentals=0)


def low_half(shape):
    return lax.broadcasted_iota(jnp.int32, shape, len(shape) - 1) < BS


def split_pair(first, second):
    low = low_half(first.shape)
    zero = jnp.where(low, first, pltpu.roll(second, BS, 1))
    one = jnp.where(low, pltpu.roll(first, BS, 1), second)
    return zero, one


def send_copies(block, out_ref):
    tile = jnp.concatenate([block[8 * i : 8 * i + 8, 0:NSNAP] for i in range(4)], axis=1)
    for p in range(out_ref.shape[0]):
        out_ref[p] = tile


def sum_copies(ref):
    parts = [ref[p] for p in range(ref.shape[0])]
    while len(parts) > 1:
        parts = [x + y for x, y in zip(parts[0::2], parts[1::2])]
    tile = parts[0]
    return jnp.concatenate([tile] + [pltpu.roll(tile, LANES - NSNAP * i, 1) for i in range(1, 4)], axis=0)


def my_part():
    return lax.axis_index("file") * lax.axis_size("rows") + lax.axis_index("rows")


def pack_kernel(map_ref, snap_hbm, out_ref, recv_ref, snap_ref, index_ref, rows_ref, snap_sem, rows_sem):
    fetch = pltpu.make_async_copy(snap_hbm, snap_ref, snap_sem)
    fetch.start()
    n_part, slots = map_ref.shape
    per_pair = out_ref.shape[1] // 4
    held = slots * per_pair

    local = map_ref[...] - lax.axis_index("rows") * held
    group = local >> 7
    within = (local & 127).astype(jnp.float32)
    ones = jnp.ones((8, slots), jnp.bfloat16)
    for q in range(per_pair):
        part = jnp.where(group == q, within, 0.0).astype(jnp.bfloat16)
        found = lax.dot_general(ones, part, NT, preferred_element_type=jnp.float32)
        row = found[0:1].astype(jnp.int32) + q * slots
        index_ref[q : q + 1, :] = (row >> 3) * 32 + (row & 7)
    move = pltpu.make_async_copy(index_ref, rows_ref, rows_sem)
    move.start()

    mine = map_ref[pl.ds(my_part(), 1), :]
    recv_ref[...] = (mine >> 9) * (4 * per_pair) + ((mine >> 7) & (per_pair - 1)) * 4
    move.wait()
    fetch.wait()

    def body(part, carry):
        for q in range(per_pair):
            row = rows_ref[q, part]
            out_ref[part, 4 * q : 4 * q + 4, :] = snap_ref[pl.ds(row, 4, stride=8), :]
        return carry

    lax.fori_loop(0, n_part, body, 0, unroll=8)


def pack(snapshots, part_map, n_part):
    blocks, width = snapshots.shape
    tiles = width // LANES
    slots = part_map.shape[0] // n_part
    per_pair = blocks // slots
    assert slots == 128 and tiles == 4 and per_pair == 4
    view = snapshots.reshape(blocks // 8, 8, tiles, LANES).transpose(0, 2, 1, 3)
    view = view.reshape(blocks * tiles, LANES)
    return pl.pallas_call(
        pack_kernel,
        out_shape=(
            jax.ShapeDtypeStruct((n_part, per_pair * tiles, LANES), jnp.float32),
            jax.ShapeDtypeStruct((1, slots), jnp.int32),
        ),
        in_specs=[spec(VMEM), spec(pl.ANY)],
        out_specs=(spec(VMEM), spec(VMEM)),
        scratch_shapes=[
            pltpu.VMEM(view.shape, jnp.float32),
            pltpu.VMEM((per_pair, n_part), jnp.int32),
            pltpu.SMEM((per_pair, n_part), jnp.int32),
            pltpu.SemaphoreType.DMA,
            pltpu.SemaphoreType.DMA,
        ],
        compiler_params=limit(60),
        name="pack",
    )(part_map.reshape(n_part, slots), view)


def split_kernel(jac_ref, high_ref, low_ref):
    def body(s, carry):
        for pair in range(NNZB // 2):
            for tb in range(2):
                first = jac_ref[s, pl.ds(tb * 128 + 2 * pair, 16, stride=8), :]
                second = jac_ref[s, pl.ds(tb * 128 + 2 * pair + 1, 16, stride=8), :]
                for r2, part in enumerate(split_pair(first, second)):
                    high = part.astype(jnp.bfloat16)
                    low = (part - high.astype(jnp.float32)).astype(jnp.bfloat16)
                    rows = slice(32 * r2 + 16 * tb, 32 * r2 + 16 * tb + 16)
                    lanes = slice(LANES * pair, LANES * pair + LANES)
                    high_ref[s, rows, lanes] = high
                    low_ref[s, rows, lanes] = low
        return carry

    lax.fori_loop(0, jac_ref.shape[0], body, 0, unroll=4)


def split_blocks(jac_blocks):
    slots = jac_blocks.shape[0]
    view = jac_blocks.reshape(slots, NNZB, BS * BS // LANES, LANES).transpose(0, 2, 1, 3)
    view = view.reshape(slots, NNZB * BS * BS // LANES, LANES)
    step = 32
    out = jax.ShapeDtypeStruct((slots, BS, NNZB * BS), jnp.bfloat16)
    return pl.pallas_call(
        split_kernel,
        out_shape=(out, out),
        grid=(slots // step,),
        in_specs=[pl.BlockSpec((step,) + view.shape[1:], lambda i: (i, 0, 0))],
        out_specs=[pl.BlockSpec((step,) + out.shape[1:], lambda i: (i, 0, 0))] * 2,
        compiler_params=limit(48),
        cost_estimate=cost(0, 32 * 1024 * 1024),
        name="split_blocks",
    )(view)


def assemble_kernel(rows_ref, recv_ref, snap_ref, near_ref, far_ref):
    slots = snap_ref.shape[0]
    per_file = recv_ref.shape[0] // 4

    def body(s, carry):
        row = rows_ref[0, s]
        for f in range(4):
            snap_ref[s, 4 * f : 4 * f + 4, :] = recv_ref[pl.ds(f * per_file + row, 4), :]
        return carry

    lax.fori_loop(0, slots, body, 0, unroll=8)
    odd = my_part() % 2
    near_ref[...] = snap_ref[pl.ds((1 - odd) * (slots - RIM), RIM)]
    far_ref[...] = snap_ref[pl.ds(odd * (slots - RIM), RIM)]


def assemble(received, rows, slots):
    rim = jax.ShapeDtypeStruct((RIM, HALF, LANES), jnp.float32)
    return pl.pallas_call(
        assemble_kernel,
        out_shape=(jax.ShapeDtypeStruct((slots, HALF, LANES), jnp.float32), rim, rim),
        in_specs=[spec(SMEM), spec(VMEM)],
        out_specs=(spec(VMEM),) * 3,
        compiler_params=limit(6),
        name="assemble",
    )(rows, received.reshape(-1, LANES))


def make_pairs(snap_ref, pairs_ref):
    for sp in range(snap_ref.shape[0] // 2):
        zero, one = split_pair(snap_ref[2 * sp], snap_ref[2 * sp + 1])
        pairs_ref[0:HALF, sp * LANES : sp * LANES + LANES] = zero
        pairs_ref[HALF:NSNAP, sp * LANES : sp * LANES + LANES] = one


def gram_kernel(snap_ref, copies_ref, pairs_ref):
    make_pairs(snap_ref, pairs_ref)
    pairs = pairs_ref[...]
    gram = lax.dot_general(pairs, pairs, NT, precision=HIGH, preferred_element_type=jnp.float32)
    send_copies(gram, copies_ref)


def gram_part(snaps, n_part):
    slots = snaps.shape[0]
    return pl.pallas_call(
        gram_kernel,
        out_shape=jax.ShapeDtypeStruct((n_part, 8, LANES), jnp.float32),
        in_specs=[spec(VMEM)],
        out_specs=spec(VMEM),
        scratch_shapes=[pltpu.VMEM((NSNAP, slots * BS), jnp.float32)],
        compiler_params=limit(8),
        cost_estimate=cost(2 * 6 * NSNAP * NSNAP * slots * BS, 3 * 1024 * 1024),
        name="gram_part",
    )(snaps)


CHUNK = 32


def apply_kernel(cols_ref, near_ref, own_ref, far_ref, jh_hbm, jl_hbm, out_ref, copies_ref, xh_ref, xl_ref, pairs_ref, mixed_ref, jh_ref, jl_ref, sems):
    low16 = low_half((HALF, LANES))
    low32 = low_half((NSNAP, LANES))
    slots = own_ref.shape[0]

    def fetch(c):
        rows = pl.ds(c * CHUNK, CHUNK)
        return (
            pltpu.make_async_copy(jh_hbm.at[rows], jh_ref.at[rows], sems.at[0, c]),
            pltpu.make_async_copy(jl_hbm.at[rows], jl_ref.at[rows], sems.at[1, c]),
        )

    for c in range(slots // CHUNK):
        for copy in fetch(c):
            copy.start()

    def fill(ref, base, count):
        def body(s, carry):
            x = ref[s]
            y = pltpu.roll(x, BS, 1)
            for kk, part in enumerate((jnp.where(low16, x, y), jnp.where(low16, y, x))):
                high = part.astype(jnp.bfloat16)
                low = (part - high.astype(jnp.float32)).astype(jnp.bfloat16)
                xh_ref[base + s, HALF * kk : HALF * kk + HALF, :] = high
                xl_ref[base + s, HALF * kk : HALF * kk + HALF, :] = low
            return carry

        lax.fori_loop(0, count, body, 0, unroll=8)

    odd = my_part() % 2
    first_slot = my_part() * slots - RIM
    last_row = slots + 2 * RIM - 1
    fill(near_ref, (1 - odd) * (slots + RIM), RIM)
    fill(own_ref, RIM, slots)
    fill(far_ref, odd * (slots + RIM), RIM)
    xh_ref[last_row + 1] = jnp.zeros((NSNAP, LANES), jnp.bfloat16)
    xl_ref[last_row + 1] = jnp.zeros((NSNAP, LANES), jnp.bfloat16)
    make_pairs(own_ref, pairs_ref)

    def table_row(n, s):
        column = cols_ref[n, s]
        row = jnp.minimum(jnp.maximum(column - first_slot, 0), last_row)
        return jnp.where(column < 0, last_row + 1, row)

    lane = lax.broadcasted_iota(jnp.int32, (NSNAP, LANES), 1)
    r = lane % BS
    order = lane - r + (r % 2) * (BS // 2) + r // 2
    group = 4

    def body(g, carry):
        highs, lows = [], []
        for i in range(group):
            hi_parts, lo_parts = [], []
            for pair in range(NNZB // 2):
                a = table_row(2 * pair, g * group + i)
                b = table_row(2 * pair + 1, g * group + i)
                hi_parts.append(jnp.where(low32, xh_ref[a], xh_ref[b]))
                lo_parts.append(jnp.where(low32, xl_ref[a], xl_ref[b]))
            highs.append(jnp.concatenate(hi_parts, axis=1))
            lows.append(jnp.concatenate(lo_parts, axis=1))
        high = jnp.concatenate(highs, axis=0)
        both = jnp.concatenate(highs + lows, axis=0)
        jh = jh_ref[pl.ds(g * group, group)].reshape(group * BS, NNZB * BS)
        jl = jl_ref[pl.ds(g * group, group)].reshape(group * BS, NNZB * BS)
        big = lax.dot_general(both, jh, NT, preferred_element_type=jnp.float32)
        acc = big[0 : group * NSNAP] + big[group * NSNAP :]
        acc = acc + lax.dot_general(high, jl, NT, preferred_element_type=jnp.float32)
        for ip in range(group // 2):
            tile = acc[:, LANES * ip : LANES * ip + LANES]
            top = tile[2 * ip * NSNAP : 2 * ip * NSNAP + NSNAP]
            bottom = tile[2 * ip * NSNAP + NSNAP : 2 * ip * NSNAP + 2 * NSNAP]
            mixed = jnp.take_along_axis(jnp.where(low32, top, bottom), order, axis=1)
            mixed_ref[:, pl.ds(pl.multiple_of((g * 2 + ip) * LANES, LANES), LANES)] = mixed
            first, second = split_pair(mixed[0:HALF], mixed[HALF:NSNAP])
            out_ref[g * group + 2 * ip] = first
            out_ref[g * group + 2 * ip + 1] = second
        return carry

    def chunk(c, carry):
        for copy in fetch(c):
            copy.wait()
        per_chunk = CHUNK // group
        for j in range(per_chunk):
            body(c * per_chunk + j, carry)
        return carry

    lax.fori_loop(0, slots // CHUNK, chunk, 0)
    reduced = lax.dot_general(pairs_ref[...], mixed_ref[...], NT, precision=HIGH, preferred_element_type=jnp.float32)
    send_copies(reduced, copies_ref)


def apply_blocks(cols, near, own, far, jac_high, jac_low, n_part):
    slots = own.shape[0]
    table = pltpu.VMEM((slots + 2 * RIM + 1, NSNAP, LANES), jnp.bfloat16)
    wide = pltpu.VMEM((NSNAP, slots * BS), jnp.float32)
    held = pltpu.VMEM(jac_high.shape, jac_high.dtype)
    return pl.pallas_call(
        apply_kernel,
        out_shape=(
            jax.ShapeDtypeStruct((slots, HALF, LANES), jnp.float32),
            jax.ShapeDtypeStruct((n_part, 8, LANES), jnp.float32),
        ),
        in_specs=[spec(SMEM)] + [spec(VMEM)] * 3 + [spec(pl.ANY)] * 2,
        out_specs=(spec(VMEM),) * 2,
        scratch_shapes=[table, table, wide, wide, held, held, pltpu.SemaphoreType.DMA((2, slots // CHUNK))],
        compiler_params=limit(48),
        cost_estimate=cost(2 * 3 * slots * 4 * NSNAP * 512 * BS, 24 * 1024 * 1024),
        name="apply_blocks",
    )(cols, near, own, far, jac_high, jac_low)


def factor(gram, total_rows):
    row = lax.broadcasted_iota(jnp.int32, (NSNAP, LANES), 0)
    lane = lax.broadcasted_iota(jnp.int32, (NSNAP, LANES), 1)
    rank = 2 * (row % HALF) + row // HALF
    unit = jnp.where(lane - NSNAP == row, 1.0, 0.0).astype(jnp.float32)
    work = jnp.where(lane < NSNAP, gram, unit)
    wide = lambda x: jnp.broadcast_to(x, (NSNAP, LANES))
    for k2 in range(HALF):
        p, q = k2, HALF + k2
        row_p, row_q = wide(work[p : p + 1, :]), wide(work[q : q + 1, :])
        col_p, col_q = wide(work[:, p : p + 1]), wide(work[:, q : q + 1])
        a = wide(work[p : p + 1, p : p + 1])
        b = wide(work[q : q + 1, p : p + 1])
        c = wide(work[q : q + 1, q : q + 1])
        ratio = b / a
        row_q = row_q - ratio * row_p
        below = (col_p / a) * row_p + ((col_q - ratio * col_p) / (c - ratio * b)) * row_q
        work = work - jnp.where(rank > 2 * k2 + 1, below, jnp.where(rank == 2 * k2 + 1, ratio * row_p, 0.0))
    diag = jnp.sum(jnp.where(lane == row, work, 0.0), axis=1, keepdims=True)
    scale = float(total_rows) ** 0.5 / jnp.sqrt(diag)
    return pltpu.roll(work, LANES - NSNAP, 1) * scale


def mix_kernel(total_rows, gram_ref, snap_ref, jac_ref, basis_ref, out_ref, scaled_ref, same_ref, swap_ref, plain_ref, turned_ref):
    low = low_half((HALF, LANES))

    @pl.when(pl.program_id(0) == 0)
    def _():
        scaled = factor(sum_copies(gram_ref), total_rows)
        scaled_ref[...] = scaled[:, 0:NSNAP]
        wide = lambda kk, j: jnp.broadcast_to(scaled[kk * HALF : kk * HALF + HALF, j : j + 1], (HALF, LANES))
        for j2 in range(HALF):
            same_ref[j2] = jnp.where(low, wide(0, j2), wide(1, HALF + j2))
            swap_ref[j2] = jnp.where(low, wide(0, HALF + j2), wide(1, j2))

    both = range(2)
    for source, target in ((snap_ref, basis_ref), (jac_ref, out_ref)):
        def body(pair, carry):
            for j2 in range(HALF):
                for h in both:
                    x = source[pl.ds((2 * pair + h) * 8 * HALF + j2, 8, stride=HALF), :]
                    plain_ref[h, j2] = x
                    turned_ref[h, j2] = pltpu.roll(x, BS, 1)
            for k4 in range(0, HALF, 4):
                totals = {}
                for j2 in range(k4 + 4):
                    values = [(plain_ref[h, j2], turned_ref[h, j2]) for h in both]
                    for k2 in range(max(k4, j2), k4 + 4):
                        same = jnp.broadcast_to(same_ref[j2, k2 : k2 + 1, :], (8, LANES))
                        swap = jnp.broadcast_to(swap_ref[j2, k2 : k2 + 1, :], (8, LANES))
                        for h in both:
                            term = same * values[h][0] + swap * values[h][1]
                            totals[k2, h] = totals[k2, h] + term if j2 else term
                for k2 in range(k4, k4 + 4):
                    for h in both:
                        rows = pl.ds(pl.multiple_of((2 * pair + h) * 8, 8), 8)
                        target[rows, LANES * k2 : LANES * k2 + LANES] = totals[k2, h]
            return carry

        lax.fori_loop(0, target.shape[0] // 16, body, 0)


def mix(gram, snaps, jac, total_rows):
    slots = snaps.shape[0]
    step = 32
    out = jax.ShapeDtypeStruct((slots, NSNAP * BS), jnp.float32)
    flat = lambda x: x.reshape(slots * HALF, LANES)
    rows = pl.BlockSpec((step * HALF, LANES), lambda i: (i, 0))
    return pl.pallas_call(
        lambda *refs: mix_kernel(total_rows, *refs),
        out_shape=(out, out, jax.ShapeDtypeStruct((NSNAP, NSNAP), jnp.float32)),
        grid=(slots // step,),
        in_specs=[pl.BlockSpec(gram.shape, lambda i: (0, 0, 0)), rows, rows],
        out_specs=[pl.BlockSpec((step, NSNAP * BS), lambda i: (i, 0))] * 2 + [pl.BlockSpec((NSNAP, NSNAP), lambda i: (0, 0))],
        scratch_shapes=[pltpu.VMEM((HALF, HALF, LANES), jnp.float32)] * 2 + [pltpu.VMEM((2, HALF, 8, LANES), jnp.float32)] * 2,
        cost_estimate=cost(2 * 2 * slots * BS * NSNAP * NSNAP, 4 * 1024 * 1024),
        compiler_params=limit(12),
        name="mix",
    )(gram, flat(snaps), flat(jac))


def finish_kernel(total_rows, scaled_ref, red_ref, out_ref):
    row = lax.broadcasted_iota(jnp.int32, (NSNAP, NSNAP), 0)
    col = lax.broadcasted_iota(jnp.int32, (NSNAP, NSNAP), 1)
    place = jnp.where(col == (row % 2) * HALF + row // 2, 1.0, 0.0).astype(jnp.float32)
    dot = lambda a, b, dims: lax.dot_general(a, b, dims, precision=HIGH, preferred_element_type=jnp.float32)
    nn = (((1,), (0,)), ((), ()))
    natural = dot(place, scaled_ref[...], nn)
    reduced = sum_copies(red_ref)[:, 0:NSNAP]
    out_ref[...] = dot(dot(natural, reduced, nn), natural, NT) / float(total_rows)


def finish(scaled, reduced, total_rows):
    return pl.pallas_call(
        lambda *refs: finish_kernel(total_rows, *refs),
        out_shape=jax.ShapeDtypeStruct((NSNAP, NSNAP), jnp.float32),
        in_specs=[spec(VMEM)] * 2,
        out_specs=spec(VMEM),
        compiler_params=limit(4),
        name="finish",
    )(scaled, reduced)


def exchange(tiles):
    return lax.all_to_all(tiles, AXES, split_axis=0, concat_axis=0, tiled=True)


def shards(snapshots, part_map, jac_blocks, jac_cols):
    n_part = lax.axis_size("file") * lax.axis_size("rows")
    blocks = jac_blocks.shape[0]
    total_rows = blocks * BS * n_part

    packed, recv_rows = pack(snapshots, part_map, n_part)
    received = exchange(packed)
    jac_high, jac_low = split_blocks(jac_blocks)
    received, jac_high, jac_low = lax.optimization_barrier((received, jac_high, jac_low))
    snaps, near, far = assemble(received, recv_rows, blocks)

    near_swap = [(p, p ^ 1) for p in range(n_part)]
    far_swap = [(p, ((p + 1) ^ 1) - 1) for p in range(1, n_part - 1)]
    far = lax.ppermute(far, AXES, far_swap)
    near = lax.ppermute(near, AXES, near_swap)
    gram = exchange(gram_part(snaps, n_part))
    jac_snaps, reduced_tiles = apply_blocks(jac_cols.T, near, snaps, far, jac_high, jac_low, n_part)

    reduced = exchange(reduced_tiles)
    basis, jac_basis, scaled = mix(gram, snaps, jac_snaps, total_rows)
    return basis, jac_basis, finish(scaled, reduced, total_rows)


def solution(mesh):
    in_specs = (P("rows", "file"), P(), P(AXES, None, None), P(AXES, None))
    out_specs = (P(AXES, None), P(AXES, None), P())
    return jax.shard_map(shards, mesh=mesh, in_specs=in_specs, out_specs=out_specs, check_vma=False)
```

```python
import jax
import jax.numpy as jnp
from jax import lax
from jax.experimental import pallas as pl
from jax.experimental.pallas import tpu as pltpu
from jax.sharding import PartitionSpec as P

NSNAP = 32
BS = 64
NNZB = 8
RIM = 32
HALF = NSNAP // 2
LANES = 128
AXES = ("file", "rows")
GROUP = 4
BATCH = 8
VMEM = pltpu.VMEM
SMEM = pltpu.SMEM
NT = (((1,), (1,)), ((), ()))
HIGH = lax.Precision.HIGHEST


def spec(space):
    return pl.BlockSpec(memory_space=space)


def limit(mib):
    return pltpu.CompilerParams(vmem_limit_bytes=mib * 1024 * 1024)


def cost(flops, nbytes):
    return pl.CostEstimate(flops=flops, bytes_accessed=nbytes, transcendentals=0)


def low_half(shape):
    return lax.broadcasted_iota(jnp.int32, shape, len(shape) - 1) < BS


def split_pair(first, second):
    low = low_half(first.shape)
    zero = jnp.where(low, first, pltpu.roll(second, BS, 1))
    one = jnp.where(low, pltpu.roll(first, BS, 1), second)
    return zero, one


def to_tile(block):
    return jnp.concatenate([block[8 * i : 8 * i + 8, 0:NSNAP] for i in range(4)], axis=1)


def tree_sum(parts):
    while len(parts) > 1:
        parts = [x + y for x, y in zip(parts[0::2], parts[1::2])]
    return parts[0]


def from_tile(tile):
    return [tile] + [pltpu.roll(tile, LANES - NSNAP * i, 1) for i in range(1, 4)]


def my_part():
    return lax.axis_index("file") * lax.axis_size("rows") + lax.axis_index("rows")


def pack_kernel(map_ref, cols_ref, snap_hbm, out_ref, recv_ref, snap_ref, index_ref, rows_ref, snap_sem, rows_sem):
    fetch = pltpu.make_async_copy(snap_hbm, snap_ref, snap_sem)
    fetch.start()
    n_part, slots = map_ref.shape
    per_pair = out_ref.shape[1] // 4
    held = slots * per_pair

    local = map_ref[...] - lax.axis_index("rows") * held
    group = local >> 7
    within = (local & 127).astype(jnp.float32)
    ones = jnp.ones((8, slots), jnp.bfloat16)
    for q in range(per_pair):
        part = jnp.where(group == q, within, 0.0).astype(jnp.bfloat16)
        found = lax.dot_general(ones, part, NT, preferred_element_type=jnp.float32)
        row = found[0:1].astype(jnp.int32) + q * slots
        index_ref[q : q + 1, :] = (row >> 3) * 32 + (row & 7)
    move = pltpu.make_async_copy(index_ref, rows_ref, rows_sem)
    move.start()

    mine = map_ref[pl.ds(my_part(), 1), :]
    recv_ref[0:1, :] = (mine >> 9) * (4 * per_pair) + ((mine >> 7) & (per_pair - 1)) * 4

    cols = cols_ref[...]
    start = my_part() * slots
    below = ((cols >= 0) & (cols < start)).astype(jnp.int32)
    above = (cols >= start + slots).astype(jnp.int32)
    uses_far = jnp.where(my_part() % 2 == 1, above, below)
    recv_ref[1:2, :] = jnp.max(uses_far, axis=0, keepdims=True)
    move.wait()
    fetch.wait()

    def body(part, carry):
        for q in range(per_pair):
            row = rows_ref[q, part]
            out_ref[part, 4 * q : 4 * q + 4, :] = snap_ref[pl.ds(row, 4, stride=8), :]
        return carry

    lax.fori_loop(0, n_part, body, 0, unroll=8)


def pack(snapshots, part_map, cols, n_part):
    blocks, width = snapshots.shape
    tiles = width // LANES
    slots = part_map.shape[0] // n_part
    per_pair = blocks // slots
    assert slots == 128 and tiles == 4 and per_pair == 4
    view = snapshots.reshape(blocks // 8, 8, tiles, LANES).transpose(0, 2, 1, 3)
    view = view.reshape(blocks * tiles, LANES)
    return pl.pallas_call(
        pack_kernel,
        out_shape=(
            jax.ShapeDtypeStruct((n_part, per_pair * tiles, LANES), jnp.float32),
            jax.ShapeDtypeStruct((2, slots), jnp.int32),
        ),
        in_specs=[spec(VMEM), spec(VMEM), spec(pl.ANY)],
        out_specs=(spec(VMEM), spec(VMEM)),
        scratch_shapes=[
            pltpu.VMEM(view.shape, jnp.float32),
            pltpu.VMEM((per_pair, n_part), jnp.int32),
            pltpu.SMEM((per_pair, n_part), jnp.int32),
            pltpu.SemaphoreType.DMA,
            pltpu.SemaphoreType.DMA,
        ],
        compiler_params=limit(60),
        name="pack",
    )(part_map.reshape(n_part, slots), cols, view)


def order_groups(flags_ref, order_ref):
    count = order_ref.shape[0] - 1

    def body(g, found):
        at = g * GROUP
        far = flags_ref[1, at]
        for i in range(1, GROUP):
            far = far | flags_ref[1, at + i]
        order_ref[jnp.where(far == 1, count - 1 - (g - found), found)] = g
        return found + 1 - far

    order_ref[count] = lax.fori_loop(0, count, body, jnp.int32(0)) // BATCH


def split_kernel(flags_ref, jac_ref, out_ref, order_ref):
    @pl.when(pl.program_id(0) == 0)
    def _():
        order_groups(flags_ref, order_ref)

    def body(s, carry):
        for pair in range(NNZB // 2):
            for tb in range(2):
                first = jac_ref[s, pl.ds(tb * 128 + 2 * pair, 16, stride=8), :]
                second = jac_ref[s, pl.ds(tb * 128 + 2 * pair + 1, 16, stride=8), :]
                for r2, part in enumerate(split_pair(first, second)):
                    high = part.astype(jnp.bfloat16)
                    low = (part - high.astype(jnp.float32)).astype(jnp.bfloat16)
                    rows = slice(32 * r2 + 16 * tb, 32 * r2 + 16 * tb + 16)
                    lanes = slice(LANES * pair, LANES * pair + LANES)
                    out_ref[s, 0, rows, lanes] = high
                    out_ref[s, 1, rows, lanes] = low
        return carry

    lax.fori_loop(0, jac_ref.shape[0], body, 0, unroll=4)


def split_blocks(jac_blocks, flags):
    slots = jac_blocks.shape[0]
    view = jac_blocks.reshape(slots, NNZB, BS * BS // LANES, LANES).transpose(0, 2, 1, 3)
    view = view.reshape(slots, NNZB * BS * BS // LANES, LANES)
    step = 32
    out = jax.ShapeDtypeStruct((slots, 2, BS, NNZB * BS), jnp.bfloat16)
    return pl.pallas_call(
        split_kernel,
        out_shape=(out, jax.ShapeDtypeStruct((slots // GROUP + 1,), jnp.int32)),
        grid=(slots // step,),
        in_specs=[spec(SMEM), pl.BlockSpec((step,) + view.shape[1:], lambda i: (i, 0, 0))],
        out_specs=(pl.BlockSpec((step,) + out.shape[1:], lambda i: (i, 0, 0, 0)), spec(SMEM)),
        compiler_params=limit(48),
        cost_estimate=cost(0, 32 * 1024 * 1024),
        name="split_blocks",
    )(flags, view)


def assemble_kernel(rows_ref, recv_ref, snap_ref, near_ref, far_ref):
    slots = snap_ref.shape[0]
    per_file = recv_ref.shape[0] // 4

    def body(s, carry):
        row = rows_ref[0, s]
        for f in range(4):
            snap_ref[s, 4 * f : 4 * f + 4, :] = recv_ref[pl.ds(f * per_file + row, 4), :]
        return carry

    lax.fori_loop(0, slots, body, 0, unroll=8)
    odd = my_part() % 2
    near_ref[...] = snap_ref[pl.ds((1 - odd) * (slots - RIM), RIM)]
    far_ref[...] = snap_ref[pl.ds(odd * (slots - RIM), RIM)]


def assemble(received, rows, slots):
    rim = jax.ShapeDtypeStruct((RIM, HALF, LANES), jnp.float32)
    return pl.pallas_call(
        assemble_kernel,
        out_shape=(jax.ShapeDtypeStruct((slots, HALF, LANES), jnp.float32), rim, rim),
        in_specs=[spec(SMEM), spec(VMEM)],
        out_specs=(spec(VMEM),) * 3,
        compiler_params=limit(6),
        name="assemble",
    )(rows, received.reshape(-1, LANES))


def make_pairs(snap_ref, pairs_ref):
    for sp in range(snap_ref.shape[0] // 2):
        zero, one = split_pair(snap_ref[2 * sp], snap_ref[2 * sp + 1])
        pairs_ref[0:HALF, sp * LANES : sp * LANES + LANES] = zero
        pairs_ref[HALF:NSNAP, sp * LANES : sp * LANES + LANES] = one


def gram_kernel(snap_ref, tile_ref, pairs_ref):
    make_pairs(snap_ref, pairs_ref)
    pairs = pairs_ref[...]
    gram = lax.dot_general(pairs, pairs, NT, precision=HIGH, preferred_element_type=jnp.float32)
    tile_ref[...] = to_tile(gram)


def gram_part(snaps):
    slots = snaps.shape[0]
    return pl.pallas_call(
        gram_kernel,
        out_shape=jax.ShapeDtypeStruct((8, LANES), jnp.float32),
        in_specs=[spec(VMEM)],
        out_specs=spec(VMEM),
        scratch_shapes=[pltpu.VMEM((NSNAP, slots * BS), jnp.float32)],
        compiler_params=limit(8),
        cost_estimate=cost(2 * 6 * NSNAP * NSNAP * slots * BS, 3 * 1024 * 1024),
        name="gram_part",
    )(snaps)


def fill(ref, xh_ref, xl_ref, base):
    low = low_half((HALF, LANES))

    def body(s, carry):
        x = ref[s]
        y = pltpu.roll(x, BS, 1)
        for kk, part in enumerate((jnp.where(low, x, y), jnp.where(low, y, x))):
            high = part.astype(jnp.bfloat16)
            rest = (part - high.astype(jnp.float32)).astype(jnp.bfloat16)
            xh_ref[base + s, HALF * kk : HALF * kk + HALF, :] = high
            xl_ref[base + s, HALF * kk : HALF * kk + HALF, :] = rest
        return carry

    lax.fori_loop(0, ref.shape[0], body, 0, unroll=8)


def run_batches(first, last, cols_ref, own_ref, jac_hbm, out_ref, red_ref, xh_ref, xl_ref, jac_ref, order_ref, sems, prepare):
    slots = own_ref.shape[0]
    low32 = low_half((NSNAP, LANES))
    lane = lax.broadcasted_iota(jnp.int32, (NSNAP, LANES), 1)
    r = lane % BS
    lanes = lane - r + (r % 2) * (BS // 2) + r // 2
    first_slot = my_part() * slots - RIM
    last_row = slots + 2 * RIM - 1

    def fetch(at):
        source = pl.ds(order_ref[at] * GROUP, GROUP)
        target = pl.ds(at * GROUP, GROUP)
        return pltpu.make_async_copy(jac_hbm.at[source], jac_ref.at[target], sems.at[at])

    def start(at, carry):
        fetch(at).start()
        return carry

    lax.fori_loop(first * BATCH, last * BATCH, start, 0)
    prepare()

    def table_row(n, s):
        column = cols_ref[n, s]
        row = jnp.minimum(jnp.maximum(column - first_slot, 0), last_row)
        return jnp.where(column < 0, last_row + 1, row)

    def product(at):
        g = order_ref[at]
        highs, lows = [], []
        for i in range(GROUP):
            hi_parts, lo_parts = [], []
            for pair in range(NNZB // 2):
                a = table_row(2 * pair, g * GROUP + i)
                b = table_row(2 * pair + 1, g * GROUP + i)
                hi_parts.append(jnp.where(low32, xh_ref[a], xh_ref[b]))
                lo_parts.append(jnp.where(low32, xl_ref[a], xl_ref[b]))
            highs.append(jnp.concatenate(hi_parts, axis=1))
            lows.append(jnp.concatenate(lo_parts, axis=1))
        high = jnp.concatenate(highs, axis=0)
        both = jnp.concatenate(highs + lows, axis=0)
        rows = pl.ds(at * GROUP, GROUP)
        jh = jac_ref[rows, 0].reshape(GROUP * BS, NNZB * BS)
        jl = jac_ref[rows, 1].reshape(GROUP * BS, NNZB * BS)
        big = lax.dot_general(both, jh, NT, preferred_element_type=jnp.float32)
        acc = big[0 : GROUP * NSNAP] + big[GROUP * NSNAP :]
        acc = acc + lax.dot_general(high, jl, NT, preferred_element_type=jnp.float32)
        results, pairs = [], []
        for ip in range(GROUP // 2):
            tile = acc[:, LANES * ip : LANES * ip + LANES]
            top = tile[2 * ip * NSNAP : 2 * ip * NSNAP + NSNAP]
            bottom = tile[2 * ip * NSNAP + NSNAP : 2 * ip * NSNAP + 2 * NSNAP]
            mixed = jnp.take_along_axis(jnp.where(low32, top, bottom), lanes, axis=1)
            s = g * GROUP + 2 * ip
            out_ref[s], out_ref[s + 1] = split_pair(mixed[0:HALF], mixed[HALF:NSNAP])
            results.append(mixed)
            pairs.append(jnp.concatenate(split_pair(own_ref[s], own_ref[s + 1]), axis=0))
        return pairs, results

    red_ref[...] = jnp.zeros_like(red_ref)

    def batch(b, carry):
        for j in range(BATCH):
            fetch(b * BATCH + j).wait()
        pairs, results = [], []
        for j in range(BATCH):
            x, y = product(b * BATCH + j)
            pairs += x
            results += y
        red_ref[...] += lax.dot_general(
            jnp.concatenate(pairs, axis=1),
            jnp.concatenate(results, axis=1),
            NT,
            precision=HIGH,
            preferred_element_type=jnp.float32,
        )
        return carry

    lax.fori_loop(first, last, batch, 0)


def fill_zero(xh_ref, xl_ref):
    xh_ref[xh_ref.shape[0] - 1] = jnp.zeros(xh_ref.shape[1:], jnp.bfloat16)
    xl_ref[xl_ref.shape[0] - 1] = jnp.zeros(xl_ref.shape[1:], jnp.bfloat16)


def near_kernel(order_ref, cols_ref, near_ref, own_ref, jac_hbm, out_ref, red_ref, xh_ref, xl_ref, jac_ref, sems):
    slots = own_ref.shape[0]
    odd = my_part() % 2

    def prepare():
        fill(near_ref, xh_ref, xl_ref, (1 - odd) * (slots + RIM))
        fill(own_ref, xh_ref, xl_ref, RIM)
        fill_zero(xh_ref, xl_ref)

    batches = order_ref[slots // GROUP]
    run_batches(0, batches, cols_ref, own_ref, jac_hbm, out_ref, red_ref, xh_ref, xl_ref, jac_ref, order_ref, sems, prepare)


def far_kernel(order_ref, cols_ref, near_ref, far_ref, own_ref, gram_ref, done_ref, red_in_ref, jac_hbm, out_ref, keep_ref, give_ref, red_ref, xh_ref, xl_ref, jac_ref, sems):
    slots = own_ref.shape[0]
    odd = my_part() % 2

    def prepare():
        out_ref[...] = done_ref[...]
        fill(near_ref, xh_ref, xl_ref, (1 - odd) * (slots + RIM))
        fill(own_ref, xh_ref, xl_ref, RIM)
        fill(far_ref, xh_ref, xl_ref, odd * (slots + RIM))
        fill_zero(xh_ref, xl_ref)

    batches = order_ref[slots // GROUP]
    last = slots // GROUP // BATCH
    run_batches(batches, last, cols_ref, own_ref, jac_hbm, out_ref, red_ref, xh_ref, xl_ref, jac_ref, order_ref, sems, prepare)

    gram = gram_ref[...]
    reduced = to_tile(red_in_ref[...] + red_ref[...])
    keep_ref[...] = jnp.where(odd == 1, reduced, gram)
    give_ref[...] = jnp.where(odd == 1, gram, reduced)


def scratch(slots, jac_split):
    table = pltpu.VMEM((slots + 2 * RIM + 1, NSNAP, LANES), jnp.bfloat16)
    return [table, table, pltpu.VMEM(jac_split.shape, jac_split.dtype), pltpu.SemaphoreType.DMA((slots // GROUP,))]


def apply_near(order, cols, near, own, jac_split):
    slots = own.shape[0]
    return pl.pallas_call(
        near_kernel,
        out_shape=(
            jax.ShapeDtypeStruct((slots, HALF, LANES), jnp.float32),
            jax.ShapeDtypeStruct((NSNAP, NSNAP), jnp.float32),
        ),
        in_specs=[spec(SMEM)] * 2 + [spec(VMEM)] * 2 + [spec(pl.ANY)],
        out_specs=(spec(VMEM),) * 2,
        scratch_shapes=scratch(slots, jac_split),
        compiler_params=limit(50),
        cost_estimate=cost(2 * 3 * slots * 3 * NSNAP * 512 * BS, 20 * 1024 * 1024),
        name="apply_near",
    )(order, cols, near, own, jac_split)


def apply_far(order, cols, near, far, own, gram, done, jac_split):
    slots = own.shape[0]
    tile = jax.ShapeDtypeStruct((8, LANES), jnp.float32)
    return pl.pallas_call(
        far_kernel,
        out_shape=(jax.ShapeDtypeStruct((slots, HALF, LANES), jnp.float32), tile, tile),
        in_specs=[spec(SMEM)] * 2 + [spec(VMEM)] * 6 + [spec(pl.ANY)],
        out_specs=(spec(VMEM),) * 3,
        scratch_shapes=[pltpu.VMEM((NSNAP, NSNAP), jnp.float32)] + scratch(slots, jac_split),
        compiler_params=limit(50),
        cost_estimate=cost(2 * 3 * slots * NSNAP * 512 * BS, 8 * 1024 * 1024),
        name="apply_far",
    )(order, cols, near, far, own, gram, *done, jac_split)


def factor(gram, total_rows):
    groups = range(NSNAP // 8)
    row = lax.broadcasted_iota(jnp.int32, (8, LANES), 0)
    lane = lax.broadcasted_iota(jnp.int32, (8, LANES), 1)
    rank = [2 * ((row + 8 * v) % HALF) + (row + 8 * v) // HALF for v in groups]
    work = [
        jnp.where(lane < NSNAP, gram[v], jnp.where(lane - NSNAP == row + 8 * v, 1.0, 0.0).astype(jnp.float32))
        for v in groups
    ]
    row_of = lambda x, p: jnp.broadcast_to(x[p // 8][p % 8 : p % 8 + 1, :], (8, LANES))
    step = 4
    for first in range(0, NSNAP, step):
        at = [(k % 2) * HALF + k // 2 for k in range(first, first + step)]
        rows = [row_of(work, p) for p in at]
        cols = [[jnp.broadcast_to(x[:, p : p + 1], (8, LANES)) for x in work] for p in at]
        block = [[row_of(cols[n], at[m]) for n in range(step)] for m in range(step)]
        below = [jnp.zeros((8, LANES), jnp.float32) for _ in groups]
        for m in range(step):
            inverse = 1.0 / block[m][m]
            for v in groups:
                ratio = cols[m][v] * inverse
                below[v] = below[v] + ratio * rows[m]
                for n in range(m + 1, step):
                    cols[n][v] = cols[n][v] - ratio * block[m][n]
            for n in range(m + 1, step):
                ratio = block[n][m] * inverse
                rows[n] = rows[n] - ratio * rows[m]
                block[n] = [x - ratio * y for x, y in zip(block[n], block[m])]
        for v in groups:
            new = jnp.where(rank[v] >= first + step, work[v] - below[v], work[v])
            for m in range(step):
                if at[m] // 8 == v:
                    new = jnp.where(row == at[m] % 8, rows[m], new)
            work[v] = new
    scaled = []
    for v in groups:
        diag = jnp.sum(jnp.where(lane == row + 8 * v, work[v], 0.0), axis=1, keepdims=True)
        scaled.append(pltpu.roll(work[v], LANES - NSNAP, 1) * (float(total_rows) ** 0.5 / jnp.sqrt(diag)))
    return jnp.concatenate(scaled, axis=0)


def finish(scaled, reduced):
    row = lax.broadcasted_iota(jnp.int32, (NSNAP, NSNAP), 0)
    col = lax.broadcasted_iota(jnp.int32, (NSNAP, NSNAP), 1)
    place = jnp.where(col == (row % 2) * HALF + row // 2, 1.0, 0.0).astype(jnp.float32)
    dot = lambda a, b, dims: lax.dot_general(a, b, dims, precision=HIGH, preferred_element_type=jnp.float32)
    nn = (((1,), (0,)), ((), ()))
    natural = dot(place, scaled, nn)
    return dot(dot(natural, reduced, nn), natural, NT)


def mix_kernel(total_rows, sums_ref, snap_ref, jac_ref, basis_ref, out_ref, final_ref, same_ref, swap_ref, plain_ref, turned_ref):
    low = low_half((HALF, LANES))

    @pl.when(pl.program_id(0) == 0)
    def _():
        n_part = sums_ref.shape[0]
        gram = tree_sum([sums_ref[p] for p in range(0, n_part, 2)])
        scaled = factor(from_tile(gram), total_rows)
        reduced = tree_sum([sums_ref[p] for p in range(1, n_part, 2)])
        reduced = jnp.concatenate(from_tile(reduced), axis=0)[:, 0:NSNAP]
        final_ref[...] = finish(scaled[:, 0:NSNAP], reduced) / float(total_rows)
        wide = lambda kk, j: jnp.broadcast_to(scaled[kk * HALF : kk * HALF + HALF, j : j + 1], (HALF, LANES))
        for j2 in range(HALF):
            same_ref[j2] = jnp.where(low, wide(0, j2), wide(1, HALF + j2))
            swap_ref[j2] = jnp.where(low, wide(0, HALF + j2), wide(1, j2))

    both = range(2)
    for source, target in ((snap_ref, basis_ref), (jac_ref, out_ref)):
        def body(pair, carry):
            for j2 in range(HALF):
                for h in both:
                    x = source[pl.ds((2 * pair + h) * 8 * HALF + j2, 8, stride=HALF), :]
                    plain_ref[h, j2] = x
                    turned_ref[h, j2] = pltpu.roll(x, BS, 1)
            for k4 in range(0, HALF, 4):
                totals = {}
                for j2 in range(k4 + 4):
                    values = [(plain_ref[h, j2], turned_ref[h, j2]) for h in both]
                    for k2 in range(max(k4, j2), k4 + 4):
                        same = jnp.broadcast_to(same_ref[j2, k2 : k2 + 1, :], (8, LANES))
                        swap = jnp.broadcast_to(swap_ref[j2, k2 : k2 + 1, :], (8, LANES))
                        for h in both:
                            term = same * values[h][0] + swap * values[h][1]
                            totals[k2, h] = totals[k2, h] + term if j2 else term
                for k2 in range(k4, k4 + 4):
                    for h in both:
                        rows = pl.ds(pl.multiple_of((2 * pair + h) * 8, 8), 8)
                        target[rows, LANES * k2 : LANES * k2 + LANES] = totals[k2, h]
            return carry

        lax.fori_loop(0, target.shape[0] // 16, body, 0)


def mix(sums, snaps, jac, total_rows):
    slots = snaps.shape[0]
    step = 32
    out = jax.ShapeDtypeStruct((slots, NSNAP * BS), jnp.float32)
    flat = lambda x: x.reshape(slots * HALF, LANES)
    rows = pl.BlockSpec((step * HALF, LANES), lambda i: (i, 0))
    return pl.pallas_call(
        lambda *refs: mix_kernel(total_rows, *refs),
        out_shape=(out, out, jax.ShapeDtypeStruct((NSNAP, NSNAP), jnp.float32)),
        grid=(slots // step,),
        in_specs=[pl.BlockSpec(sums.shape, lambda i: (0, 0, 0)), rows, rows],
        out_specs=[pl.BlockSpec((step, NSNAP * BS), lambda i: (i, 0))] * 2 + [pl.BlockSpec((NSNAP, NSNAP), lambda i: (0, 0))],
        scratch_shapes=[pltpu.VMEM((HALF, HALF, LANES), jnp.float32)] * 2 + [pltpu.VMEM((2, HALF, 8, LANES), jnp.float32)] * 2,
        cost_estimate=cost(2 * 2 * slots * BS * NSNAP * NSNAP, 4 * 1024 * 1024),
        compiler_params=limit(12),
        name="mix",
    )(sums, flat(snaps), flat(jac))


def exchange(tiles):
    return lax.all_to_all(tiles, AXES, split_axis=0, concat_axis=0, tiled=True)


def shards(snapshots, part_map, jac_blocks, jac_cols):
    n_part = lax.axis_size("file") * lax.axis_size("rows")
    blocks = jac_blocks.shape[0]
    total_rows = blocks * BS * n_part

    cols = jac_cols.T
    packed, table = pack(snapshots, part_map, cols, n_part)
    received = exchange(packed)
    jac_split, order = split_blocks(jac_blocks, table)
    received, jac_split, order = lax.optimization_barrier((received, jac_split, order))
    snaps, near, far = assemble(received, table, blocks)

    near_swap = [(p, p ^ 1) for p in range(n_part)]
    far_swap = [(p, ((p + 1) ^ 1) - 1) for p in range(1, n_part - 1)]
    far = lax.ppermute(far, AXES, far_swap)
    near = lax.ppermute(near, AXES, near_swap)
    gram = gram_part(snaps)
    done = apply_near(order, cols, near, snaps, jac_split)
    done, far = lax.optimization_barrier((done, far))
    jac_snaps, keep, give = apply_far(order, cols, near, far, snaps, gram, done, jac_split)
    pair_sum = keep + lax.ppermute(give, AXES, near_swap)
    sums = exchange(jnp.broadcast_to(pair_sum[None], (n_part, 8, LANES)))
    return mix(sums, snaps, jac_snaps, total_rows)


def solution(mesh):
    in_specs = (P("rows", "file"), P(), P(AXES, None, None), P(AXES, None))
    out_specs = (P(AXES, None), P(AXES, None), P())
    return jax.shard_map(shards, mesh=mesh, in_specs=in_specs, out_specs=out_specs, check_vma=False)
```

```python
import jax
import jax.numpy as jnp
from jax import lax
from jax.experimental import pallas as pl
from jax.experimental.pallas import tpu as pltpu
from jax.sharding import PartitionSpec as P

NSNAP = 32
BS = 64
NNZB = 8
RIM = 32
HALF = NSNAP // 2
LANES = 128
AXES = ("file", "rows")
GROUP = 4
BATCH = 8
VMEM = pltpu.VMEM
SMEM = pltpu.SMEM
NT = (((1,), (1,)), ((), ()))
HIGH = lax.Precision.HIGHEST


def spec(space):
    return pl.BlockSpec(memory_space=space)


def limit(mib):
    return pltpu.CompilerParams(vmem_limit_bytes=mib * 1024 * 1024)


def cost(flops, nbytes):
    return pl.CostEstimate(flops=flops, bytes_accessed=nbytes, transcendentals=0)


def low_half(shape):
    return lax.broadcasted_iota(jnp.int32, shape, len(shape) - 1) < BS


def split_pair(first, second):
    low = low_half(first.shape)
    zero = jnp.where(low, first, pltpu.roll(second, BS, 1))
    one = jnp.where(low, pltpu.roll(first, BS, 1), second)
    return zero, one


def to_tile(block):
    return jnp.concatenate([block[8 * i : 8 * i + 8, 0:NSNAP] for i in range(4)], axis=1)


def tree_sum(parts):
    while len(parts) > 1:
        parts = [x + y for x, y in zip(parts[0::2], parts[1::2])]
    return parts[0]


def from_tile(tile):
    return [tile] + [pltpu.roll(tile, LANES - NSNAP * i, 1) for i in range(1, 4)]


def my_part():
    return lax.axis_index("file") * lax.axis_size("rows") + lax.axis_index("rows")


def pack_kernel(map_ref, cols_ref, snap_hbm, out_ref, recv_ref, snap_ref, index_ref, rows_ref, snap_sem, rows_sem):
    fetch = pltpu.make_async_copy(snap_hbm, snap_ref, snap_sem)
    fetch.start()
    n_part, slots = map_ref.shape
    per_pair = out_ref.shape[1] // 4
    held = slots * per_pair

    local = map_ref[...] - lax.axis_index("rows") * held
    group = local >> 7
    within = (local & 127).astype(jnp.float32)
    ones = jnp.ones((8, slots), jnp.bfloat16)
    for q in range(per_pair):
        part = jnp.where(group == q, within, 0.0).astype(jnp.bfloat16)
        found = lax.dot_general(ones, part, NT, preferred_element_type=jnp.float32)
        row = found[0:1].astype(jnp.int32) + q * slots
        index_ref[q : q + 1, :] = (row >> 3) * 32 + (row & 7)
    move = pltpu.make_async_copy(index_ref, rows_ref, rows_sem)
    move.start()

    mine = map_ref[pl.ds(my_part(), 1), :]
    recv_ref[0:1, :] = (mine >> 9) * (4 * per_pair) + ((mine >> 7) & (per_pair - 1)) * 4

    cols = cols_ref[...]
    start = my_part() * slots
    below = ((cols >= 0) & (cols < start)).astype(jnp.int32)
    above = (cols >= start + slots).astype(jnp.int32)
    uses_far = jnp.where(my_part() % 2 == 1, above, below)
    recv_ref[1:2, :] = jnp.max(uses_far, axis=0, keepdims=True)
    move.wait()
    fetch.wait()

    def body(part, carry):
        for q in range(per_pair):
            row = rows_ref[q, part]
            out_ref[part, 4 * q : 4 * q + 4, :] = snap_ref[pl.ds(row, 4, stride=8), :]
        return carry

    lax.fori_loop(0, n_part, body, 0, unroll=8)


def pack(snapshots, part_map, cols, n_part):
    blocks, width = snapshots.shape
    tiles = width // LANES
    slots = part_map.shape[0] // n_part
    per_pair = blocks // slots
    assert slots == 128 and tiles == 4 and per_pair == 4
    view = snapshots.reshape(blocks // 8, 8, tiles, LANES).transpose(0, 2, 1, 3)
    view = view.reshape(blocks * tiles, LANES)
    return pl.pallas_call(
        pack_kernel,
        out_shape=(
            jax.ShapeDtypeStruct((n_part, per_pair * tiles, LANES), jnp.float32),
            jax.ShapeDtypeStruct((2, slots), jnp.int32),
        ),
        in_specs=[spec(VMEM), spec(VMEM), spec(pl.ANY)],
        out_specs=(spec(VMEM), spec(VMEM)),
        scratch_shapes=[
            pltpu.VMEM(view.shape, jnp.float32),
            pltpu.VMEM((per_pair, n_part), jnp.int32),
            pltpu.SMEM((per_pair, n_part), jnp.int32),
            pltpu.SemaphoreType.DMA,
            pltpu.SemaphoreType.DMA,
        ],
        compiler_params=limit(60),
        name="pack",
    )(part_map.reshape(n_part, slots), cols, view)


def order_groups(flags_ref, order_ref):
    count = order_ref.shape[0] - 1

    def body(g, found):
        at = g * GROUP
        far = flags_ref[1, at]
        for i in range(1, GROUP):
            far = far | flags_ref[1, at + i]
        order_ref[jnp.where(far == 1, count - 1 - (g - found), found)] = g
        return found + 1 - far

    order_ref[count] = lax.fori_loop(0, count, body, jnp.int32(0)) // BATCH


def split_kernel(flags_ref, jac_ref, out_ref, order_ref):
    @pl.when(pl.program_id(0) == 0)
    def _():
        order_groups(flags_ref, order_ref)

    def body(s, carry):
        for pair in range(NNZB // 2):
            for tb in range(2):
                first = jac_ref[s, pl.ds(tb * 128 + 2 * pair, 16, stride=8), :]
                second = jac_ref[s, pl.ds(tb * 128 + 2 * pair + 1, 16, stride=8), :]
                for r2, part in enumerate(split_pair(first, second)):
                    high = part.astype(jnp.bfloat16)
                    low = (part - high.astype(jnp.float32)).astype(jnp.bfloat16)
                    rows = slice(32 * r2 + 16 * tb, 32 * r2 + 16 * tb + 16)
                    lanes = slice(LANES * pair, LANES * pair + LANES)
                    out_ref[s, 0, rows, lanes] = high
                    out_ref[s, 1, rows, lanes] = low
        return carry

    lax.fori_loop(0, jac_ref.shape[0], body, 0, unroll=4)


def split_blocks(jac_blocks, flags):
    slots = jac_blocks.shape[0]
    view = jac_blocks.reshape(slots, NNZB, BS * BS // LANES, LANES).transpose(0, 2, 1, 3)
    view = view.reshape(slots, NNZB * BS * BS // LANES, LANES)
    step = 32
    out = jax.ShapeDtypeStruct((slots, 2, BS, NNZB * BS), jnp.bfloat16)
    return pl.pallas_call(
        split_kernel,
        out_shape=(out, jax.ShapeDtypeStruct((slots // GROUP + 1,), jnp.int32)),
        grid=(slots // step,),
        in_specs=[spec(SMEM), pl.BlockSpec((step,) + view.shape[1:], lambda i: (i, 0, 0))],
        out_specs=(pl.BlockSpec((step,) + out.shape[1:], lambda i: (i, 0, 0, 0)), spec(SMEM)),
        compiler_params=limit(48),
        cost_estimate=cost(0, 32 * 1024 * 1024),
        name="split_blocks",
    )(flags, view)


def assemble_kernel(rows_ref, recv_ref, snap_ref, near_ref, far_ref):
    slots = snap_ref.shape[0]
    per_file = recv_ref.shape[0] // 4

    def body(s, carry):
        row = rows_ref[0, s]
        for f in range(4):
            snap_ref[s, 4 * f : 4 * f + 4, :] = recv_ref[pl.ds(f * per_file + row, 4), :]
        return carry

    lax.fori_loop(0, slots, body, 0, unroll=8)
    odd = my_part() % 2
    near_ref[...] = snap_ref[pl.ds((1 - odd) * (slots - RIM), RIM)]
    far_ref[...] = snap_ref[pl.ds(odd * (slots - RIM), RIM)]


def assemble(received, rows, slots):
    rim = jax.ShapeDtypeStruct((RIM, HALF, LANES), jnp.float32)
    return pl.pallas_call(
        assemble_kernel,
        out_shape=(jax.ShapeDtypeStruct((slots, HALF, LANES), jnp.float32), rim, rim),
        in_specs=[spec(SMEM), spec(VMEM)],
        out_specs=(spec(VMEM),) * 3,
        compiler_params=limit(6),
        name="assemble",
    )(rows, received.reshape(-1, LANES))


def make_pairs(snap_ref, pairs_ref):
    for sp in range(snap_ref.shape[0] // 2):
        zero, one = split_pair(snap_ref[2 * sp], snap_ref[2 * sp + 1])
        pairs_ref[0:HALF, sp * LANES : sp * LANES + LANES] = zero
        pairs_ref[HALF:NSNAP, sp * LANES : sp * LANES + LANES] = one


def fill(ref, xh_ref, xl_ref, base):
    low = low_half((HALF, LANES))

    def body(s, carry):
        x = ref[s]
        y = pltpu.roll(x, BS, 1)
        for kk, part in enumerate((jnp.where(low, x, y), jnp.where(low, y, x))):
            high = part.astype(jnp.bfloat16)
            rest = (part - high.astype(jnp.float32)).astype(jnp.bfloat16)
            xh_ref[base + s, HALF * kk : HALF * kk + HALF, :] = high
            xl_ref[base + s, HALF * kk : HALF * kk + HALF, :] = rest
        return carry

    lax.fori_loop(0, ref.shape[0], body, 0, unroll=8)


def run_batches(first, last, cols_ref, own_ref, jac_hbm, out_ref, red_ref, xh_ref, xl_ref, jac_ref, order_ref, sems, prepare):
    slots = own_ref.shape[0]
    low32 = low_half((NSNAP, LANES))
    lane = lax.broadcasted_iota(jnp.int32, (NSNAP, LANES), 1)
    r = lane % BS
    lanes = lane - r + (r % 2) * (BS // 2) + r // 2
    first_slot = my_part() * slots - RIM
    last_row = slots + 2 * RIM - 1

    def fetch(at):
        source = pl.ds(order_ref[at] * GROUP, GROUP)
        target = pl.ds(at * GROUP, GROUP)
        return pltpu.make_async_copy(jac_hbm.at[source], jac_ref.at[target], sems.at[at])

    def start(at, carry):
        fetch(at).start()
        return carry

    lax.fori_loop(first * BATCH, jnp.minimum(first + 1, last) * BATCH, start, 0)
    prepare()

    def table_row(n, s):
        column = cols_ref[n, s]
        row = jnp.minimum(jnp.maximum(column - first_slot, 0), last_row)
        return jnp.where(column < 0, last_row + 1, row)

    def product(at):
        g = order_ref[at]
        highs, lows = [], []
        for i in range(GROUP):
            hi_parts, lo_parts = [], []
            for pair in range(NNZB // 2):
                a = table_row(2 * pair, g * GROUP + i)
                b = table_row(2 * pair + 1, g * GROUP + i)
                hi_parts.append(jnp.where(low32, xh_ref[a], xh_ref[b]))
                lo_parts.append(jnp.where(low32, xl_ref[a], xl_ref[b]))
            highs.append(jnp.concatenate(hi_parts, axis=1))
            lows.append(jnp.concatenate(lo_parts, axis=1))
        high = jnp.concatenate(highs, axis=0)
        both = jnp.concatenate(highs + lows, axis=0)
        rows = pl.ds(at * GROUP, GROUP)
        jh = jac_ref[rows, 0].reshape(GROUP * BS, NNZB * BS)
        jl = jac_ref[rows, 1].reshape(GROUP * BS, NNZB * BS)
        big = lax.dot_general(both, jh, NT, preferred_element_type=jnp.float32)
        acc = big[0 : GROUP * NSNAP] + big[GROUP * NSNAP :]
        acc = acc + lax.dot_general(high, jl, NT, preferred_element_type=jnp.float32)
        results, pairs = [], []
        for ip in range(GROUP // 2):
            tile = acc[:, LANES * ip : LANES * ip + LANES]
            top = tile[2 * ip * NSNAP : 2 * ip * NSNAP + NSNAP]
            bottom = tile[2 * ip * NSNAP + NSNAP : 2 * ip * NSNAP + 2 * NSNAP]
            mixed = jnp.take_along_axis(jnp.where(low32, top, bottom), lanes, axis=1)
            s = g * GROUP + 2 * ip
            out_ref[s], out_ref[s + 1] = split_pair(mixed[0:HALF], mixed[HALF:NSNAP])
            results.append(mixed)
            pairs.append(jnp.concatenate(split_pair(own_ref[s], own_ref[s + 1]), axis=0))
        return pairs, results

    red_ref[...] = jnp.zeros_like(red_ref)

    def batch(b, carry):
        lax.fori_loop((b + 1) * BATCH, jnp.minimum(b + 2, last) * BATCH, start, 0)
        for j in range(BATCH):
            fetch(b * BATCH + j).wait()
        pairs, results = [], []
        for j in range(BATCH):
            x, y = product(b * BATCH + j)
            pairs += x
            results += y
        red_ref[...] += lax.dot_general(
            jnp.concatenate(pairs, axis=1),
            jnp.concatenate(results, axis=1),
            NT,
            precision=HIGH,
            preferred_element_type=jnp.float32,
        )
        return carry

    lax.fori_loop(first, last, batch, 0)


def fill_zero(xh_ref, xl_ref):
    xh_ref[xh_ref.shape[0] - 1] = jnp.zeros(xh_ref.shape[1:], jnp.bfloat16)
    xl_ref[xl_ref.shape[0] - 1] = jnp.zeros(xl_ref.shape[1:], jnp.bfloat16)


def near_kernel(order_ref, cols_ref, near_ref, own_ref, jac_hbm, out_ref, red_ref, xh_ref, xl_ref, jac_ref, sems):
    slots = own_ref.shape[0]
    odd = my_part() % 2

    def prepare():
        fill(near_ref, xh_ref, xl_ref, (1 - odd) * (slots + RIM))
        fill(own_ref, xh_ref, xl_ref, RIM)
        fill_zero(xh_ref, xl_ref)

    batches = order_ref[slots // GROUP]
    run_batches(0, batches, cols_ref, own_ref, jac_hbm, out_ref, red_ref, xh_ref, xl_ref, jac_ref, order_ref, sems, prepare)


def far_kernel(order_ref, cols_ref, far_ref, own_ref, done_ref, red_in_ref, th_ref, tl_ref, jac_hbm, out_ref, keep_ref, give_ref, red_ref, gram_ref, pairs_ref, table_sems, xh_ref, xl_ref, jac_ref, sems):
    slots = own_ref.shape[0]
    odd = my_part() % 2

    def prepare():
        copies = (
            pltpu.make_async_copy(th_ref, xh_ref, table_sems.at[0]),
            pltpu.make_async_copy(tl_ref, xl_ref, table_sems.at[1]),
            pltpu.make_async_copy(done_ref, out_ref, table_sems.at[2]),
        )
        for copy in copies:
            copy.start()
        make_pairs(own_ref, pairs_ref)
        pairs = pairs_ref[...]
        gram_ref[...] = lax.dot_general(pairs, pairs, NT, precision=HIGH, preferred_element_type=jnp.float32)
        for copy in copies:
            copy.wait()
        fill(far_ref, xh_ref, xl_ref, odd * (slots + RIM))

    batches = order_ref[slots // GROUP]
    last = slots // GROUP // BATCH
    run_batches(batches, last, cols_ref, own_ref, jac_hbm, out_ref, red_ref, xh_ref, xl_ref, jac_ref, order_ref, sems, prepare)

    gram = to_tile(gram_ref[...])
    reduced = to_tile(red_in_ref[...] + red_ref[...])
    keep_ref[...] = jnp.where(odd == 1, reduced, gram)
    give_ref[...] = jnp.where(odd == 1, gram, reduced)


def apply_near(order, cols, near, own, jac_split):
    slots = own.shape[0]
    table = jax.ShapeDtypeStruct((slots + 2 * RIM + 1, NSNAP, LANES), jnp.bfloat16)
    return pl.pallas_call(
        near_kernel,
        out_shape=(
            jax.ShapeDtypeStruct((slots, HALF, LANES), jnp.float32),
            jax.ShapeDtypeStruct((NSNAP, NSNAP), jnp.float32),
            table,
            table,
        ),
        in_specs=[spec(SMEM)] * 2 + [spec(VMEM)] * 2 + [spec(pl.ANY)],
        out_specs=(spec(VMEM),) * 4,
        scratch_shapes=[
            pltpu.VMEM(jac_split.shape, jac_split.dtype),
            pltpu.SemaphoreType.DMA((slots // GROUP,)),
        ],
        compiler_params=limit(46),
        cost_estimate=cost(2 * 3 * slots * 3 * NSNAP * 512 * BS, 20 * 1024 * 1024),
        name="apply_near",
    )(order, cols, near, own, jac_split)


def apply_far(order, cols, far, own, done, jac_split):
    slots = own.shape[0]
    tile = jax.ShapeDtypeStruct((8, LANES), jnp.float32)
    table = pltpu.VMEM(done[2].shape, done[2].dtype)
    return pl.pallas_call(
        far_kernel,
        out_shape=(jax.ShapeDtypeStruct((slots, HALF, LANES), jnp.float32), tile, tile),
        in_specs=[spec(SMEM)] * 2 + [spec(VMEM)] * 6 + [spec(pl.ANY)],
        out_specs=(spec(VMEM),) * 3,
        scratch_shapes=[
            pltpu.VMEM((NSNAP, NSNAP), jnp.float32),
            pltpu.VMEM((NSNAP, NSNAP), jnp.float32),
            pltpu.VMEM((NSNAP, slots * BS), jnp.float32),
            pltpu.SemaphoreType.DMA((3,)),
            table,
            table,
            pltpu.VMEM(jac_split.shape, jac_split.dtype),
            pltpu.SemaphoreType.DMA((slots // GROUP,)),
        ],
        compiler_params=limit(46),
        cost_estimate=cost(2 * 3 * slots * NSNAP * 512 * BS, 8 * 1024 * 1024),
        name="apply_far",
    )(order, cols, far, own, *done, jac_split)


def factor(gram, total_rows):
    groups = range(NSNAP // 8)
    row = lax.broadcasted_iota(jnp.int32, (8, LANES), 0)
    lane = lax.broadcasted_iota(jnp.int32, (8, LANES), 1)
    rank = [2 * ((row + 8 * v) % HALF) + (row + 8 * v) // HALF for v in groups]
    work = [
        jnp.where(lane < NSNAP, gram[v], jnp.where(lane - NSNAP == row + 8 * v, 1.0, 0.0).astype(jnp.float32))
        for v in groups
    ]
    row_of = lambda x, p: jnp.broadcast_to(x[p // 8][p % 8 : p % 8 + 1, :], (8, LANES))
    step = 8
    for first in range(0, NSNAP, step):
        at = [(k % 2) * HALF + k // 2 for k in range(first, first + step)]
        rows = [row_of(work, p) for p in at]
        cols = [[jnp.broadcast_to(x[:, p : p + 1], (8, LANES)) for x in work] for p in at]
        block = [[row_of(cols[n], at[m]) for n in range(step)] for m in range(step)]
        below = [jnp.zeros((8, LANES), jnp.float32) for _ in groups]
        for m in range(step):
            inverse = 1.0 / block[m][m]
            for v in groups:
                ratio = cols[m][v] * inverse
                below[v] = below[v] + ratio * rows[m]
                for n in range(m + 1, step):
                    cols[n][v] = cols[n][v] - ratio * block[m][n]
            for n in range(m + 1, step):
                ratio = block[n][m] * inverse
                rows[n] = rows[n] - ratio * rows[m]
                block[n] = [x - ratio * y for x, y in zip(block[n], block[m])]
        for v in groups:
            new = jnp.where(rank[v] >= first + step, work[v] - below[v], work[v])
            for m in range(step):
                if at[m] // 8 == v:
                    new = jnp.where(row == at[m] % 8, rows[m], new)
            work[v] = new
    scaled = []
    for v in groups:
        diag = jnp.sum(jnp.where(lane == row + 8 * v, work[v], 0.0), axis=1, keepdims=True)
        scaled.append(pltpu.roll(work[v], LANES - NSNAP, 1) * (float(total_rows) ** 0.5 / jnp.sqrt(diag)))
    return jnp.concatenate(scaled, axis=0)


def finish(scaled, reduced):
    row = lax.broadcasted_iota(jnp.int32, (NSNAP, NSNAP), 0)
    col = lax.broadcasted_iota(jnp.int32, (NSNAP, NSNAP), 1)
    place = jnp.where(col == (row % 2) * HALF + row // 2, 1.0, 0.0).astype(jnp.float32)
    dot = lambda a, b, dims: lax.dot_general(a, b, dims, precision=HIGH, preferred_element_type=jnp.float32)
    nn = (((1,), (0,)), ((), ()))
    natural = dot(place, scaled, nn)
    return dot(dot(natural, reduced, nn), natural, NT)


def mix_kernel(total_rows, sums_ref, snap_ref, jac_ref, basis_ref, out_ref, final_ref, same_ref, swap_ref, plain_ref, turned_ref):
    low = low_half((HALF, LANES))

    @pl.when(pl.program_id(0) == 0)
    def _():
        n_part = sums_ref.shape[0]
        gram = tree_sum([sums_ref[p] for p in range(0, n_part, 2)])
        scaled = factor(from_tile(gram), total_rows)
        reduced = tree_sum([sums_ref[p] for p in range(1, n_part, 2)])
        reduced = jnp.concatenate(from_tile(reduced), axis=0)[:, 0:NSNAP]
        final_ref[...] = finish(scaled[:, 0:NSNAP], reduced) / float(total_rows)
        wide = lambda kk, j: jnp.broadcast_to(scaled[kk * HALF : kk * HALF + HALF, j : j + 1], (HALF, LANES))
        for j2 in range(HALF):
            same_ref[j2] = jnp.where(low, wide(0, j2), wide(1, HALF + j2))
            swap_ref[j2] = jnp.where(low, wide(0, HALF + j2), wide(1, j2))

    both = range(2)
    for source, target in ((snap_ref, basis_ref), (jac_ref, out_ref)):
        def body(pair, carry):
            for j2 in range(HALF):
                for h in both:
                    x = source[pl.ds((2 * pair + h) * 8 * HALF + j2, 8, stride=HALF), :]
                    plain_ref[h, j2] = x
                    turned_ref[h, j2] = pltpu.roll(x, BS, 1)
            for k4 in range(0, HALF, 4):
                totals = {}
                for j2 in range(k4 + 4):
                    values = [(plain_ref[h, j2], turned_ref[h, j2]) for h in both]
                    for k2 in range(max(k4, j2), k4 + 4):
                        same = jnp.broadcast_to(same_ref[j2, k2 : k2 + 1, :], (8, LANES))
                        swap = jnp.broadcast_to(swap_ref[j2, k2 : k2 + 1, :], (8, LANES))
                        for h in both:
                            term = same * values[h][0] + swap * values[h][1]
                            totals[k2, h] = totals[k2, h] + term if j2 else term
                for k2 in range(k4, k4 + 4):
                    for h in both:
                        rows = pl.ds(pl.multiple_of((2 * pair + h) * 8, 8), 8)
                        target[rows, LANES * k2 : LANES * k2 + LANES] = totals[k2, h]
            return carry

        lax.fori_loop(0, target.shape[0] // 16, body, 0)


def mix(sums, snaps, jac, total_rows):
    slots = snaps.shape[0]
    step = 32
    out = jax.ShapeDtypeStruct((slots, NSNAP * BS), jnp.float32)
    flat = lambda x: x.reshape(slots * HALF, LANES)
    rows = pl.BlockSpec((step * HALF, LANES), lambda i: (i, 0))
    return pl.pallas_call(
        lambda *refs: mix_kernel(total_rows, *refs),
        out_shape=(out, out, jax.ShapeDtypeStruct((NSNAP, NSNAP), jnp.float32)),
        grid=(slots // step,),
        in_specs=[pl.BlockSpec(sums.shape, lambda i: (0, 0, 0)), rows, rows],
        out_specs=[pl.BlockSpec((step, NSNAP * BS), lambda i: (i, 0))] * 2 + [pl.BlockSpec((NSNAP, NSNAP), lambda i: (0, 0))],
        scratch_shapes=[pltpu.VMEM((HALF, HALF, LANES), jnp.float32)] * 2 + [pltpu.VMEM((2, HALF, 8, LANES), jnp.float32)] * 2,
        cost_estimate=cost(2 * 2 * slots * BS * NSNAP * NSNAP, 4 * 1024 * 1024),
        compiler_params=limit(12),
        name="mix",
    )(sums, flat(snaps), flat(jac))


def exchange(tiles):
    return lax.all_to_all(tiles, AXES, split_axis=0, concat_axis=0, tiled=True)


def shards(snapshots, part_map, jac_blocks, jac_cols):
    n_part = lax.axis_size("file") * lax.axis_size("rows")
    blocks = jac_blocks.shape[0]
    total_rows = blocks * BS * n_part

    cols = jac_cols.T
    packed, table = pack(snapshots, part_map, cols, n_part)
    received = exchange(packed)
    jac_split, order = split_blocks(jac_blocks, table)
    received, jac_split, order = lax.optimization_barrier((received, jac_split, order))
    snaps, near, far = assemble(received, table, blocks)

    near_swap = [(p, p ^ 1) for p in range(n_part)]
    far_swap = [(p, ((p + 1) ^ 1) - 1) for p in range(1, n_part - 1)]
    far = lax.ppermute(far, AXES, far_swap)
    near = lax.ppermute(near, AXES, near_swap)
    done = apply_near(order, cols, near, snaps, jac_split)
    done, far = lax.optimization_barrier((done, far))
    jac_snaps, keep, give = apply_far(order, cols, far, snaps, done, jac_split)
    pair_sum = keep + lax.ppermute(give, AXES, near_swap)
    sums = exchange(jnp.broadcast_to(pair_sum[None], (n_part, 8, LANES)))
    return mix(sums, snaps, jac_snaps, total_rows)


def solution(mesh):
    in_specs = (P("rows", "file"), P(), P(AXES, None, None), P(AXES, None))
    out_specs = (P(AXES, None), P(AXES, None), P())
    return jax.shard_map(shards, mesh=mesh, in_specs=in_specs, out_specs=out_specs, check_vma=False)
```

```python
import jax
import jax.numpy as jnp
from jax import lax
from jax.experimental import pallas as pl
from jax.experimental.pallas import tpu as pltpu
from jax.sharding import PartitionSpec as P

NSNAP = 32
BS = 64
NNZB = 8
RIM = 32
HALF = NSNAP // 2
LANES = 128
AXES = ("file", "rows")
GROUP = 4
BATCH = 8
VMEM = pltpu.VMEM
SMEM = pltpu.SMEM
NT = (((1,), (1,)), ((), ()))
HIGH = lax.Precision.HIGHEST


def spec(space):
    return pl.BlockSpec(memory_space=space)


def limit(mib):
    return pltpu.CompilerParams(vmem_limit_bytes=mib * 1024 * 1024)


def cost(flops, nbytes):
    return pl.CostEstimate(flops=flops, bytes_accessed=nbytes, transcendentals=0)


def low_half(shape):
    return lax.broadcasted_iota(jnp.int32, shape, len(shape) - 1) < BS


def split_pair(first, second):
    low = low_half(first.shape)
    zero = jnp.where(low, first, pltpu.roll(second, BS, 1))
    one = jnp.where(low, pltpu.roll(first, BS, 1), second)
    return zero, one


def to_tile(block):
    return jnp.concatenate([block[8 * i : 8 * i + 8, 0:NSNAP] for i in range(4)], axis=1)


def tree_sum(parts):
    while len(parts) > 1:
        parts = [x + y for x, y in zip(parts[0::2], parts[1::2])]
    return parts[0]


def from_tile(tile):
    return [tile] + [pltpu.roll(tile, LANES - NSNAP * i, 1) for i in range(1, 4)]


def my_part():
    return lax.axis_index("file") * lax.axis_size("rows") + lax.axis_index("rows")


def pack_kernel(map_ref, cols_ref, snap_hbm, out_ref, recv_ref, snap_ref, index_ref, rows_ref, snap_sem, rows_sem):
    fetch = pltpu.make_async_copy(snap_hbm, snap_ref, snap_sem)
    fetch.start()
    n_part, slots = map_ref.shape
    per_pair = out_ref.shape[1] // 4
    held = slots * per_pair

    local = map_ref[...] - lax.axis_index("rows") * held
    group = local >> 7
    within = (local & 127).astype(jnp.float32)
    ones = jnp.ones((8, slots), jnp.bfloat16)
    for q in range(per_pair):
        part = jnp.where(group == q, within, 0.0).astype(jnp.bfloat16)
        found = lax.dot_general(ones, part, NT, preferred_element_type=jnp.float32)
        row = found[0:1].astype(jnp.int32) + q * slots
        index_ref[q : q + 1, :] = (row >> 3) * 32 + (row & 7)
    move = pltpu.make_async_copy(index_ref, rows_ref, rows_sem)
    move.start()

    mine = map_ref[pl.ds(my_part(), 1), :]
    recv_ref[0:1, :] = (mine >> 9) * (4 * per_pair) + ((mine >> 7) & (per_pair - 1)) * 4

    cols = cols_ref[...]
    start = my_part() * slots
    below = ((cols >= 0) & (cols < start)).astype(jnp.int32)
    above = (cols >= start + slots).astype(jnp.int32)
    uses_far = jnp.where(my_part() % 2 == 1, above, below)
    recv_ref[1:2, :] = jnp.max(uses_far, axis=0, keepdims=True)
    move.wait()
    fetch.wait()

    def body(part, carry):
        for q in range(per_pair):
            row = rows_ref[q, part]
            out_ref[part, 4 * q : 4 * q + 4, :] = snap_ref[pl.ds(row, 4, stride=8), :]
        return carry

    lax.fori_loop(0, n_part, body, 0, unroll=16)


def pack(snapshots, part_map, cols, n_part):
    blocks, width = snapshots.shape
    tiles = width // LANES
    slots = part_map.shape[0] // n_part
    per_pair = blocks // slots
    assert slots == 128 and tiles == 4 and per_pair == 4
    view = snapshots.reshape(blocks // 8, 8, tiles, LANES).transpose(0, 2, 1, 3)
    view = view.reshape(blocks * tiles, LANES)
    return pl.pallas_call(
        pack_kernel,
        out_shape=(
            jax.ShapeDtypeStruct((n_part, per_pair * tiles, LANES), jnp.float32),
            jax.ShapeDtypeStruct((2, slots), jnp.int32),
        ),
        in_specs=[spec(VMEM), spec(VMEM), spec(pl.ANY)],
        out_specs=(spec(VMEM), spec(VMEM)),
        scratch_shapes=[
            pltpu.VMEM(view.shape, jnp.float32),
            pltpu.VMEM((per_pair, n_part), jnp.int32),
            pltpu.SMEM((per_pair, n_part), jnp.int32),
            pltpu.SemaphoreType.DMA,
            pltpu.SemaphoreType.DMA,
        ],
        compiler_params=limit(60),
        name="pack",
    )(part_map.reshape(n_part, slots), cols, view)


def order_groups(flags_ref, order_ref):
    count = order_ref.shape[0] - 1

    def body(g, found):
        at = g * GROUP
        far = flags_ref[1, at]
        for i in range(1, GROUP):
            far = far | flags_ref[1, at + i]
        order_ref[jnp.where(far == 1, count - 1 - (g - found), found)] = g
        return found + 1 - far

    order_ref[count] = lax.fori_loop(0, count, body, jnp.int32(0)) // BATCH


def split_kernel(flags_ref, jac_ref, out_ref, order_ref):
    @pl.when(pl.program_id(0) == 0)
    def _():
        order_groups(flags_ref, order_ref)

    def body(s, carry):
        for pair in range(NNZB // 2):
            for tb in range(2):
                first = jac_ref[s, pl.ds(tb * 128 + 2 * pair, 16, stride=8), :]
                second = jac_ref[s, pl.ds(tb * 128 + 2 * pair + 1, 16, stride=8), :]
                for r2, part in enumerate(split_pair(first, second)):
                    high = part.astype(jnp.bfloat16)
                    low = (part - high.astype(jnp.float32)).astype(jnp.bfloat16)
                    rows = slice(32 * r2 + 16 * tb, 32 * r2 + 16 * tb + 16)
                    lanes = slice(LANES * pair, LANES * pair + LANES)
                    out_ref[s, 0, rows, lanes] = high
                    out_ref[s, 1, rows, lanes] = low
        return carry

    lax.fori_loop(0, jac_ref.shape[0], body, 0, unroll=4)


def split_blocks(jac_blocks, flags):
    slots = jac_blocks.shape[0]
    view = jac_blocks.reshape(slots, NNZB, BS * BS // LANES, LANES).transpose(0, 2, 1, 3)
    view = view.reshape(slots, NNZB * BS * BS // LANES, LANES)
    step = 32
    out = jax.ShapeDtypeStruct((slots, 2, BS, NNZB * BS), jnp.bfloat16)
    return pl.pallas_call(
        split_kernel,
        out_shape=(out, jax.ShapeDtypeStruct((slots // GROUP + 1,), jnp.int32)),
        grid=(slots // step,),
        in_specs=[spec(SMEM), pl.BlockSpec((step,) + view.shape[1:], lambda i: (i, 0, 0))],
        out_specs=(pl.BlockSpec((step,) + out.shape[1:], lambda i: (i, 0, 0, 0)), spec(SMEM)),
        compiler_params=limit(48),
        cost_estimate=cost(0, 32 * 1024 * 1024),
        name="split_blocks",
    )(flags, view)


def assemble_kernel(rows_ref, recv_ref, snap_ref, near_ref, far_ref):
    slots = snap_ref.shape[0]
    per_file = recv_ref.shape[0] // 4

    def body(s, carry):
        row = rows_ref[0, s]
        for f in range(4):
            snap_ref[s, 4 * f : 4 * f + 4, :] = recv_ref[pl.ds(f * per_file + row, 4), :]
        return carry

    lax.fori_loop(0, slots, body, 0, unroll=16)
    odd = my_part() % 2
    near_ref[...] = snap_ref[pl.ds((1 - odd) * (slots - RIM), RIM)]
    far_ref[...] = snap_ref[pl.ds(odd * (slots - RIM), RIM)]


def assemble(received, rows, slots):
    rim = jax.ShapeDtypeStruct((RIM, HALF, LANES), jnp.float32)
    return pl.pallas_call(
        assemble_kernel,
        out_shape=(jax.ShapeDtypeStruct((slots, HALF, LANES), jnp.float32), rim, rim),
        in_specs=[spec(SMEM), spec(VMEM)],
        out_specs=(spec(VMEM),) * 3,
        compiler_params=limit(6),
        name="assemble",
    )(rows, received.reshape(-1, LANES))


def make_pairs(snap_ref, pairs_ref):
    for sp in range(snap_ref.shape[0] // 2):
        zero, one = split_pair(snap_ref[2 * sp], snap_ref[2 * sp + 1])
        pairs_ref[0:HALF, sp * LANES : sp * LANES + LANES] = zero
        pairs_ref[HALF:NSNAP, sp * LANES : sp * LANES + LANES] = one


def fill(ref, xh_ref, xl_ref, base):
    low = low_half((HALF, LANES))

    def body(s, carry):
        x = ref[s]
        y = pltpu.roll(x, BS, 1)
        for kk, part in enumerate((jnp.where(low, x, y), jnp.where(low, y, x))):
            high = part.astype(jnp.bfloat16)
            rest = (part - high.astype(jnp.float32)).astype(jnp.bfloat16)
            xh_ref[base + s, HALF * kk : HALF * kk + HALF, :] = high
            xl_ref[base + s, HALF * kk : HALF * kk + HALF, :] = rest
        return carry

    lax.fori_loop(0, ref.shape[0], body, 0, unroll=8)


def run_batches(first, last, cols_ref, own_ref, jac_hbm, out_ref, red_ref, xh_ref, xl_ref, jac_ref, order_ref, sems, prepare):
    slots = own_ref.shape[0]
    low32 = low_half((NSNAP, LANES))
    lane = lax.broadcasted_iota(jnp.int32, (NSNAP, LANES), 1)
    r = lane % BS
    lanes = lane - r + (r % 2) * (BS // 2) + r // 2
    first_slot = my_part() * slots - RIM
    last_row = slots + 2 * RIM - 1

    def fetch(at):
        source = pl.ds(order_ref[at] * GROUP, GROUP)
        target = pl.ds(at * GROUP, GROUP)
        return pltpu.make_async_copy(jac_hbm.at[source], jac_ref.at[target], sems.at[at])

    def start(at, carry):
        fetch(at).start()
        return carry

    lax.fori_loop(first * BATCH, jnp.minimum(first + 1, last) * BATCH, start, 0)
    prepare()

    def table_row(n, s):
        column = cols_ref[n, s]
        row = jnp.minimum(jnp.maximum(column - first_slot, 0), last_row)
        return jnp.where(column < 0, last_row + 1, row)

    def product(at):
        g = order_ref[at]
        highs, lows = [], []
        for i in range(GROUP):
            hi_parts, lo_parts = [], []
            for pair in range(NNZB // 2):
                a = table_row(2 * pair, g * GROUP + i)
                b = table_row(2 * pair + 1, g * GROUP + i)
                hi_parts.append(jnp.where(low32, xh_ref[a], xh_ref[b]))
                lo_parts.append(jnp.where(low32, xl_ref[a], xl_ref[b]))
            highs.append(jnp.concatenate(hi_parts, axis=1))
            lows.append(jnp.concatenate(lo_parts, axis=1))
        high = jnp.concatenate(highs, axis=0)
        both = jnp.concatenate(highs + lows, axis=0)
        rows = pl.ds(at * GROUP, GROUP)
        jh = jac_ref[rows, 0].reshape(GROUP * BS, NNZB * BS)
        jl = jac_ref[rows, 1].reshape(GROUP * BS, NNZB * BS)
        big = lax.dot_general(both, jh, NT, preferred_element_type=jnp.float32)
        acc = big[0 : GROUP * NSNAP] + big[GROUP * NSNAP :]
        acc = acc + lax.dot_general(high, jl, NT, preferred_element_type=jnp.float32)
        results, pairs = [], []
        for ip in range(GROUP // 2):
            tile = acc[:, LANES * ip : LANES * ip + LANES]
            top = tile[2 * ip * NSNAP : 2 * ip * NSNAP + NSNAP]
            bottom = tile[2 * ip * NSNAP + NSNAP : 2 * ip * NSNAP + 2 * NSNAP]
            mixed = jnp.take_along_axis(jnp.where(low32, top, bottom), lanes, axis=1)
            s = g * GROUP + 2 * ip
            out_ref[s], out_ref[s + 1] = split_pair(mixed[0:HALF], mixed[HALF:NSNAP])
            results.append(mixed)
            pairs.append(jnp.concatenate(split_pair(own_ref[s], own_ref[s + 1]), axis=0))
        return pairs, results

    red_ref[...] = jnp.zeros_like(red_ref)

    def batch(b, carry):
        lax.fori_loop((b + 1) * BATCH, jnp.minimum(b + 2, last) * BATCH, start, 0)
        for j in range(BATCH):
            fetch(b * BATCH + j).wait()
        pairs, results = [], []
        for j in range(BATCH):
            x, y = product(b * BATCH + j)
            pairs += x
            results += y
        red_ref[...] += lax.dot_general(
            jnp.concatenate(pairs, axis=1),
            jnp.concatenate(results, axis=1),
            NT,
            precision=HIGH,
            preferred_element_type=jnp.float32,
        )
        return carry

    lax.fori_loop(first, last, batch, 0)


def fill_zero(xh_ref, xl_ref):
    xh_ref[xh_ref.shape[0] - 1] = jnp.zeros(xh_ref.shape[1:], jnp.bfloat16)
    xl_ref[xl_ref.shape[0] - 1] = jnp.zeros(xl_ref.shape[1:], jnp.bfloat16)


def near_kernel(order_ref, cols_ref, near_ref, own_ref, jac_hbm, out_ref, red_ref, xh_ref, xl_ref, jac_ref, sems):
    slots = own_ref.shape[0]
    odd = my_part() % 2

    def prepare():
        fill(near_ref, xh_ref, xl_ref, (1 - odd) * (slots + RIM))
        fill(own_ref, xh_ref, xl_ref, RIM)
        fill_zero(xh_ref, xl_ref)

    batches = order_ref[slots // GROUP]
    run_batches(0, batches, cols_ref, own_ref, jac_hbm, out_ref, red_ref, xh_ref, xl_ref, jac_ref, order_ref, sems, prepare)


def far_kernel(order_ref, cols_ref, far_ref, own_ref, done_ref, red_in_ref, th_ref, tl_ref, jac_hbm, out_ref, keep_ref, give_ref, red_ref, gram_ref, pairs_ref, table_sems, xh_ref, xl_ref, jac_ref, sems):
    slots = own_ref.shape[0]
    odd = my_part() % 2

    def prepare():
        copies = (
            pltpu.make_async_copy(th_ref, xh_ref, table_sems.at[0]),
            pltpu.make_async_copy(tl_ref, xl_ref, table_sems.at[1]),
            pltpu.make_async_copy(done_ref, out_ref, table_sems.at[2]),
        )
        for copy in copies:
            copy.start()
        make_pairs(own_ref, pairs_ref)
        pairs = pairs_ref[...]
        gram_ref[...] = lax.dot_general(pairs, pairs, NT, precision=HIGH, preferred_element_type=jnp.float32)
        for copy in copies:
            copy.wait()
        fill(far_ref, xh_ref, xl_ref, odd * (slots + RIM))

    batches = order_ref[slots // GROUP]
    last = slots // GROUP // BATCH
    run_batches(batches, last, cols_ref, own_ref, jac_hbm, out_ref, red_ref, xh_ref, xl_ref, jac_ref, order_ref, sems, prepare)

    gram = to_tile(gram_ref[...])
    reduced = to_tile(red_in_ref[...] + red_ref[...])
    keep_ref[...] = jnp.where(odd == 1, reduced, gram)
    give_ref[...] = jnp.where(odd == 1, gram, reduced)


def apply_near(order, cols, near, own, jac_split):
    slots = own.shape[0]
    table = jax.ShapeDtypeStruct((slots + 2 * RIM + 1, NSNAP, LANES), jnp.bfloat16)
    return pl.pallas_call(
        near_kernel,
        out_shape=(
            jax.ShapeDtypeStruct((slots, HALF, LANES), jnp.float32),
            jax.ShapeDtypeStruct((NSNAP, NSNAP), jnp.float32),
            table,
            table,
        ),
        in_specs=[spec(SMEM)] * 2 + [spec(VMEM)] * 2 + [spec(pl.ANY)],
        out_specs=(spec(VMEM),) * 4,
        scratch_shapes=[
            pltpu.VMEM(jac_split.shape, jac_split.dtype),
            pltpu.SemaphoreType.DMA((slots // GROUP,)),
        ],
        compiler_params=limit(46),
        cost_estimate=cost(2 * 3 * slots * 3 * NSNAP * 512 * BS, 20 * 1024 * 1024),
        name="apply_near",
    )(order, cols, near, own, jac_split)


def apply_far(order, cols, far, own, done, jac_split):
    slots = own.shape[0]
    tile = jax.ShapeDtypeStruct((8, LANES), jnp.float32)
    table = pltpu.VMEM(done[2].shape, done[2].dtype)
    return pl.pallas_call(
        far_kernel,
        out_shape=(jax.ShapeDtypeStruct((slots, HALF, LANES), jnp.float32), tile, tile),
        in_specs=[spec(SMEM)] * 2 + [spec(VMEM)] * 6 + [spec(pl.ANY)],
        out_specs=(spec(VMEM),) * 3,
        scratch_shapes=[
            pltpu.VMEM((NSNAP, NSNAP), jnp.float32),
            pltpu.VMEM((NSNAP, NSNAP), jnp.float32),
            pltpu.VMEM((NSNAP, slots * BS), jnp.float32),
            pltpu.SemaphoreType.DMA((3,)),
            table,
            table,
            pltpu.VMEM(jac_split.shape, jac_split.dtype),
            pltpu.SemaphoreType.DMA((slots // GROUP,)),
        ],
        compiler_params=limit(46),
        cost_estimate=cost(2 * 3 * slots * NSNAP * 512 * BS, 8 * 1024 * 1024),
        name="apply_far",
    )(order, cols, far, own, *done, jac_split)


def factor(gram, total_rows):
    groups = range(NSNAP // 8)
    row = lax.broadcasted_iota(jnp.int32, (8, LANES), 0)
    lane = lax.broadcasted_iota(jnp.int32, (8, LANES), 1)
    rank = [2 * ((row + 8 * v) % HALF) + (row + 8 * v) // HALF for v in groups]
    work = [
        jnp.where(lane < NSNAP, gram[v], jnp.where(lane - NSNAP == row + 8 * v, 1.0, 0.0).astype(jnp.float32))
        for v in groups
    ]
    row_of = lambda x, p: jnp.broadcast_to(x[p // 8][p % 8 : p % 8 + 1, :], (8, LANES))
    step = 8
    for first in range(0, NSNAP, step):
        at = [(k % 2) * HALF + k // 2 for k in range(first, first + step)]
        rows = [row_of(work, p) for p in at]
        cols = [[jnp.broadcast_to(x[:, p : p + 1], (8, LANES)) for x in work] for p in at]
        block = [[row_of(cols[n], at[m]) for n in range(step)] for m in range(step)]
        below = [jnp.zeros((8, LANES), jnp.float32) for _ in groups]
        for m in range(step):
            inverse = 1.0 / block[m][m]
            for v in groups:
                ratio = cols[m][v] * inverse
                below[v] = below[v] + ratio * rows[m]
                for n in range(m + 1, step):
                    cols[n][v] = cols[n][v] - ratio * block[m][n]
            for n in range(m + 1, step):
                ratio = block[n][m] * inverse
                rows[n] = rows[n] - ratio * rows[m]
                block[n] = [x - ratio * y for x, y in zip(block[n], block[m])]
        for v in groups:
            new = jnp.where(rank[v] >= first + step, work[v] - below[v], work[v])
            for m in range(step):
                if at[m] // 8 == v:
                    new = jnp.where(row == at[m] % 8, rows[m], new)
            work[v] = new
    scaled = []
    for v in groups:
        diag = jnp.sum(jnp.where(lane == row + 8 * v, work[v], 0.0), axis=1, keepdims=True)
        scaled.append(pltpu.roll(work[v], LANES - NSNAP, 1) * (float(total_rows) ** 0.5 / jnp.sqrt(diag)))
    return jnp.concatenate(scaled, axis=0)


def finish(scaled, reduced):
    row = lax.broadcasted_iota(jnp.int32, (NSNAP, NSNAP), 0)
    col = lax.broadcasted_iota(jnp.int32, (NSNAP, NSNAP), 1)
    place = jnp.where(col == (row % 2) * HALF + row // 2, 1.0, 0.0).astype(jnp.float32)
    dot = lambda a, b, dims: lax.dot_general(a, b, dims, precision=HIGH, preferred_element_type=jnp.float32)
    nn = (((1,), (0,)), ((), ()))
    natural = dot(place, scaled, nn)
    return dot(dot(natural, reduced, nn), natural, NT)


def mix_kernel(total_rows, sums_ref, snap_ref, jac_ref, basis_ref, out_ref, final_ref, same_ref, swap_ref, plain_ref, turned_ref):
    low = low_half((HALF, LANES))

    @pl.when(pl.program_id(0) == 0)
    def _():
        n_part = sums_ref.shape[0]
        gram = tree_sum([sums_ref[p] for p in range(0, n_part, 2)])
        scaled = factor(from_tile(gram), total_rows)
        reduced = tree_sum([sums_ref[p] for p in range(1, n_part, 2)])
        reduced = jnp.concatenate(from_tile(reduced), axis=0)[:, 0:NSNAP]
        final_ref[...] = finish(scaled[:, 0:NSNAP], reduced) / float(total_rows)
        wide = lambda kk, j: jnp.broadcast_to(scaled[kk * HALF : kk * HALF + HALF, j : j + 1], (HALF, LANES))
        for j2 in range(HALF):
            same_ref[j2] = jnp.where(low, wide(0, j2), wide(1, HALF + j2))
            swap_ref[j2] = jnp.where(low, wide(0, HALF + j2), wide(1, j2))

    both = range(2)
    for source, target in ((snap_ref, basis_ref), (jac_ref, out_ref)):
        def body(pair, carry):
            for j2 in range(HALF):
                for h in both:
                    x = source[pl.ds((2 * pair + h) * 8 * HALF + j2, 8, stride=HALF), :]
                    plain_ref[h, j2] = x
                    turned_ref[h, j2] = pltpu.roll(x, BS, 1)
            for k4 in range(0, HALF, 4):
                totals = {}
                for j2 in range(k4 + 4):
                    values = [(plain_ref[h, j2], turned_ref[h, j2]) for h in both]
                    for k2 in range(max(k4, j2), k4 + 4):
                        same = jnp.broadcast_to(same_ref[j2, k2 : k2 + 1, :], (8, LANES))
                        swap = jnp.broadcast_to(swap_ref[j2, k2 : k2 + 1, :], (8, LANES))
                        for h in both:
                            term = same * values[h][0] + swap * values[h][1]
                            totals[k2, h] = totals[k2, h] + term if j2 else term
                for k2 in range(k4, k4 + 4):
                    for h in both:
                        rows = pl.ds(pl.multiple_of((2 * pair + h) * 8, 8), 8)
                        target[rows, LANES * k2 : LANES * k2 + LANES] = totals[k2, h]
            return carry

        lax.fori_loop(0, target.shape[0] // 16, body, 0, unroll=2)


def mix(sums, snaps, jac, total_rows):
    slots = snaps.shape[0]
    step = 32
    out = jax.ShapeDtypeStruct((slots, NSNAP * BS), jnp.float32)
    flat = lambda x: x.reshape(slots * HALF, LANES)
    rows = pl.BlockSpec((step * HALF, LANES), lambda i: (i, 0))
    return pl.pallas_call(
        lambda *refs: mix_kernel(total_rows, *refs),
        out_shape=(out, out, jax.ShapeDtypeStruct((NSNAP, NSNAP), jnp.float32)),
        grid=(slots // step,),
        in_specs=[pl.BlockSpec(sums.shape, lambda i: (0, 0, 0)), rows, rows],
        out_specs=[pl.BlockSpec((step, NSNAP * BS), lambda i: (i, 0))] * 2 + [pl.BlockSpec((NSNAP, NSNAP), lambda i: (0, 0))],
        scratch_shapes=[pltpu.VMEM((HALF, HALF, LANES), jnp.float32)] * 2 + [pltpu.VMEM((2, HALF, 8, LANES), jnp.float32)] * 2,
        cost_estimate=cost(2 * 2 * slots * BS * NSNAP * NSNAP, 4 * 1024 * 1024),
        compiler_params=limit(12),
        name="mix",
    )(sums, flat(snaps), flat(jac))


def exchange(tiles):
    return lax.all_to_all(tiles, AXES, split_axis=0, concat_axis=0, tiled=True)


def shards(snapshots, part_map, jac_blocks, jac_cols):
    n_part = lax.axis_size("file") * lax.axis_size("rows")
    blocks = jac_blocks.shape[0]
    total_rows = blocks * BS * n_part

    cols = jac_cols.T
    packed, table = pack(snapshots, part_map, cols, n_part)
    received = exchange(packed)
    jac_split, order = split_blocks(jac_blocks, table)
    received, jac_split, order = lax.optimization_barrier((received, jac_split, order))
    snaps, near, far = assemble(received, table, blocks)

    near_swap = [(p, p ^ 1) for p in range(n_part)]
    far_swap = [(p, ((p + 1) ^ 1) - 1) for p in range(1, n_part - 1)]
    far = lax.ppermute(far, AXES, far_swap)
    near = lax.ppermute(near, AXES, near_swap)
    done = apply_near(order, cols, near, snaps, jac_split)
    done, far = lax.optimization_barrier((done, far))
    jac_snaps, keep, give = apply_far(order, cols, far, snaps, done, jac_split)
    pair_sum = keep + lax.ppermute(give, AXES, near_swap)
    sums = exchange(jnp.broadcast_to(pair_sum[None], (n_part, 8, LANES)))
    return mix(sums, snaps, jac_snaps, total_rows)


def solution(mesh):
    in_specs = (P("rows", "file"), P(), P(AXES, None, None), P(AXES, None))
    out_specs = (P(AXES, None), P(AXES, None), P())
    return jax.shard_map(shards, mesh=mesh, in_specs=in_specs, out_specs=out_specs, check_vma=False)
```

```python
import jax
import jax.numpy as jnp
from jax import lax
from jax.experimental import pallas as pl
from jax.experimental.pallas import tpu as pltpu
from jax.sharding import PartitionSpec as P

NSNAP = 32
BS = 64
NNZB = 8
RIM = 32
HALF = NSNAP // 2
LANES = 128
AXES = ("file", "rows")
GROUP = 4
BATCH = 8
VMEM = pltpu.VMEM
SMEM = pltpu.SMEM
NT = (((1,), (1,)), ((), ()))
HIGH = lax.Precision.HIGHEST


def spec(space):
    return pl.BlockSpec(memory_space=space)


def limit(mib):
    return pltpu.CompilerParams(vmem_limit_bytes=mib * 1024 * 1024)


def cost(flops, nbytes):
    return pl.CostEstimate(flops=flops, bytes_accessed=nbytes, transcendentals=0)


def low_half(shape):
    return lax.broadcasted_iota(jnp.int32, shape, len(shape) - 1) < BS


def split_pair(first, second):
    low = low_half(first.shape)
    zero = jnp.where(low, first, pltpu.roll(second, BS, 1))
    one = jnp.where(low, pltpu.roll(first, BS, 1), second)
    return zero, one


def to_tile(block):
    return jnp.concatenate([block[8 * i : 8 * i + 8, 0:NSNAP] for i in range(4)], axis=1)


def tree_sum(parts):
    while len(parts) > 1:
        parts = [x + y for x, y in zip(parts[0::2], parts[1::2])]
    return parts[0]


def from_tile(tile):
    return [tile] + [pltpu.roll(tile, LANES - NSNAP * i, 1) for i in range(1, 4)]


def my_part():
    return lax.axis_index("file") * lax.axis_size("rows") + lax.axis_index("rows")


def pack_kernel(map_ref, cols_ref, snap_hbm, out_ref, recv_ref, snap_ref, index_ref, rows_ref, snap_sem, rows_sem):
    fetch = pltpu.make_async_copy(snap_hbm, snap_ref, snap_sem)
    fetch.start()
    n_part, slots = map_ref.shape
    per_pair = out_ref.shape[1] // 4
    held = slots * per_pair

    local = map_ref[...] - lax.axis_index("rows") * held
    group = local >> 7
    within = (local & 127).astype(jnp.float32)
    ones = jnp.ones((8, slots), jnp.bfloat16)
    for q in range(per_pair):
        part = jnp.where(group == q, within, 0.0).astype(jnp.bfloat16)
        found = lax.dot_general(ones, part, NT, preferred_element_type=jnp.float32)
        row = found[0:1].astype(jnp.int32) + q * slots
        index_ref[q : q + 1, :] = (row >> 3) * 32 + (row & 7)
    move = pltpu.make_async_copy(index_ref, rows_ref, rows_sem)
    move.start()

    mine = map_ref[pl.ds(my_part(), 1), :]
    recv_ref[0:1, :] = (mine >> 9) * (4 * per_pair) + ((mine >> 7) & (per_pair - 1)) * 4

    cols = cols_ref[...]
    start = my_part() * slots
    below = ((cols >= 0) & (cols < start)).astype(jnp.int32)
    above = (cols >= start + slots).astype(jnp.int32)
    uses_far = jnp.where(my_part() % 2 == 1, above, below)
    recv_ref[1:2, :] = jnp.max(uses_far, axis=0, keepdims=True)
    move.wait()
    fetch.wait()

    def body(part, carry):
        for q in range(per_pair):
            row = rows_ref[q, part]
            out_ref[part, 4 * q : 4 * q + 4, :] = snap_ref[pl.ds(row, 4, stride=8), :]
        return carry

    lax.fori_loop(0, n_part, body, 0, unroll=16)


def pack(snapshots, part_map, cols, n_part):
    blocks, width = snapshots.shape
    tiles = width // LANES
    slots = part_map.shape[0] // n_part
    per_pair = blocks // slots
    assert slots == 128 and tiles == 4 and per_pair == 4
    view = snapshots.reshape(blocks // 8, 8, tiles, LANES).transpose(0, 2, 1, 3)
    view = view.reshape(blocks * tiles, LANES)
    return pl.pallas_call(
        pack_kernel,
        out_shape=(
            jax.ShapeDtypeStruct((n_part, per_pair * tiles, LANES), jnp.float32),
            jax.ShapeDtypeStruct((2, slots), jnp.int32),
        ),
        in_specs=[spec(VMEM), spec(VMEM), spec(pl.ANY)],
        out_specs=(spec(VMEM), spec(VMEM)),
        scratch_shapes=[
            pltpu.VMEM(view.shape, jnp.float32),
            pltpu.VMEM((per_pair, n_part), jnp.int32),
            pltpu.SMEM((per_pair, n_part), jnp.int32),
            pltpu.SemaphoreType.DMA,
            pltpu.SemaphoreType.DMA,
        ],
        compiler_params=limit(60),
        name="pack",
    )(part_map.reshape(n_part, slots), cols, view)


def order_groups(flags_ref, order_ref):
    count = order_ref.shape[0] - 1

    def body(g, found):
        at = g * GROUP
        far = flags_ref[1, at]
        for i in range(1, GROUP):
            far = far | flags_ref[1, at + i]
        order_ref[jnp.where(far == 1, count - 1 - (g - found), found)] = g
        return found + 1 - far

    order_ref[count] = lax.fori_loop(0, count, body, jnp.int32(0)) // BATCH


def split_kernel(flags_ref, jac_ref, out_ref, order_ref):
    @pl.when(pl.program_id(0) == 0)
    def _():
        order_groups(flags_ref, order_ref)

    def body(s, carry):
        for pair in range(NNZB // 2):
            for tb in range(2):
                first = jac_ref[s, pl.ds(tb * 128 + 2 * pair, 16, stride=8), :]
                second = jac_ref[s, pl.ds(tb * 128 + 2 * pair + 1, 16, stride=8), :]
                for r2, part in enumerate(split_pair(first, second)):
                    high = part.astype(jnp.bfloat16)
                    low = (part - high.astype(jnp.float32)).astype(jnp.bfloat16)
                    rows = slice(32 * r2 + 16 * tb, 32 * r2 + 16 * tb + 16)
                    lanes = slice(LANES * pair, LANES * pair + LANES)
                    out_ref[s, 0, rows, lanes] = high
                    out_ref[s, 1, rows, lanes] = low
        return carry

    lax.fori_loop(0, jac_ref.shape[0], body, 0, unroll=8)


def split_blocks(jac_blocks, flags):
    slots = jac_blocks.shape[0]
    view = jac_blocks.reshape(slots, NNZB, BS * BS // LANES, LANES).transpose(0, 2, 1, 3)
    view = view.reshape(slots, NNZB * BS * BS // LANES, LANES)
    step = 32
    out = jax.ShapeDtypeStruct((slots, 2, BS, NNZB * BS), jnp.bfloat16)
    return pl.pallas_call(
        split_kernel,
        out_shape=(out, jax.ShapeDtypeStruct((slots // GROUP + 1,), jnp.int32)),
        grid=(slots // step,),
        in_specs=[spec(SMEM), pl.BlockSpec((step,) + view.shape[1:], lambda i: (i, 0, 0))],
        out_specs=(pl.BlockSpec((step,) + out.shape[1:], lambda i: (i, 0, 0, 0)), spec(SMEM)),
        compiler_params=limit(48),
        cost_estimate=cost(0, 32 * 1024 * 1024),
        name="split_blocks",
    )(flags, view)


def assemble_kernel(rows_ref, recv_ref, snap_ref, near_ref, far_ref):
    slots = snap_ref.shape[0]
    per_file = recv_ref.shape[0] // 4

    def body(s, carry):
        row = rows_ref[0, s]
        for f in range(4):
            snap_ref[s, 4 * f : 4 * f + 4, :] = recv_ref[pl.ds(f * per_file + row, 4), :]
        return carry

    lax.fori_loop(0, slots, body, 0, unroll=16)
    odd = my_part() % 2
    near_ref[...] = snap_ref[pl.ds((1 - odd) * (slots - RIM), RIM)]
    far_ref[...] = snap_ref[pl.ds(odd * (slots - RIM), RIM)]


def assemble(received, rows, slots):
    rim = jax.ShapeDtypeStruct((RIM, HALF, LANES), jnp.float32)
    return pl.pallas_call(
        assemble_kernel,
        out_shape=(jax.ShapeDtypeStruct((slots, HALF, LANES), jnp.float32), rim, rim),
        in_specs=[spec(SMEM), spec(VMEM)],
        out_specs=(spec(VMEM),) * 3,
        compiler_params=limit(6),
        name="assemble",
    )(rows, received.reshape(-1, LANES))


def make_pairs(snap_ref, pairs_ref):
    for sp in range(snap_ref.shape[0] // 2):
        zero, one = split_pair(snap_ref[2 * sp], snap_ref[2 * sp + 1])
        pairs_ref[0:HALF, sp * LANES : sp * LANES + LANES] = zero
        pairs_ref[HALF:NSNAP, sp * LANES : sp * LANES + LANES] = one


def fill(ref, xh_ref, xl_ref, base):
    low = low_half((HALF, LANES))

    def body(s, carry):
        x = ref[s]
        y = pltpu.roll(x, BS, 1)
        for kk, part in enumerate((jnp.where(low, x, y), jnp.where(low, y, x))):
            high = part.astype(jnp.bfloat16)
            rest = (part - high.astype(jnp.float32)).astype(jnp.bfloat16)
            xh_ref[base + s, HALF * kk : HALF * kk + HALF, :] = high
            xl_ref[base + s, HALF * kk : HALF * kk + HALF, :] = rest
        return carry

    lax.fori_loop(0, ref.shape[0], body, 0, unroll=8)


def run_batches(first, last, cols_ref, own_ref, jac_hbm, out_ref, red_ref, xh_ref, xl_ref, jac_ref, order_ref, sems, prepare):
    slots = own_ref.shape[0]
    low32 = low_half((NSNAP, LANES))
    lane = lax.broadcasted_iota(jnp.int32, (NSNAP, LANES), 1)
    r = lane % BS
    lanes = lane - r + (r % 2) * (BS // 2) + r // 2
    first_slot = my_part() * slots - RIM
    last_row = slots + 2 * RIM - 1

    def fetch(at):
        source = pl.ds(order_ref[at] * GROUP, GROUP)
        target = pl.ds(at * GROUP, GROUP)
        return pltpu.make_async_copy(jac_hbm.at[source], jac_ref.at[target], sems.at[at])

    def start(at, carry):
        fetch(at).start()
        return carry

    lax.fori_loop(first * BATCH, jnp.minimum(first + 1, last) * BATCH, start, 0)
    prepare()

    def table_row(n, s):
        column = cols_ref[n, s]
        row = jnp.minimum(jnp.maximum(column - first_slot, 0), last_row)
        return jnp.where(column < 0, last_row + 1, row)

    def product(at):
        g = order_ref[at]
        highs, lows = [], []
        for i in range(GROUP):
            hi_parts, lo_parts = [], []
            for pair in range(NNZB // 2):
                a = table_row(2 * pair, g * GROUP + i)
                b = table_row(2 * pair + 1, g * GROUP + i)
                hi_parts.append(jnp.where(low32, xh_ref[a], xh_ref[b]))
                lo_parts.append(jnp.where(low32, xl_ref[a], xl_ref[b]))
            highs.append(jnp.concatenate(hi_parts, axis=1))
            lows.append(jnp.concatenate(lo_parts, axis=1))
        high = jnp.concatenate(highs, axis=0)
        both = jnp.concatenate(highs + lows, axis=0)
        rows = pl.ds(at * GROUP, GROUP)
        jh = jac_ref[rows, 0].reshape(GROUP * BS, NNZB * BS)
        jl = jac_ref[rows, 1].reshape(GROUP * BS, NNZB * BS)
        big = lax.dot_general(both, jh, NT, preferred_element_type=jnp.float32)
        acc = big[0 : GROUP * NSNAP] + big[GROUP * NSNAP :]
        acc = acc + lax.dot_general(high, jl, NT, preferred_element_type=jnp.float32)
        results, pairs = [], []
        for ip in range(GROUP // 2):
            tile = acc[:, LANES * ip : LANES * ip + LANES]
            top = tile[2 * ip * NSNAP : 2 * ip * NSNAP + NSNAP]
            bottom = tile[2 * ip * NSNAP + NSNAP : 2 * ip * NSNAP + 2 * NSNAP]
            mixed = jnp.take_along_axis(jnp.where(low32, top, bottom), lanes, axis=1)
            s = g * GROUP + 2 * ip
            out_ref[s], out_ref[s + 1] = split_pair(mixed[0:HALF], mixed[HALF:NSNAP])
            results.append(mixed)
            pairs.append(jnp.concatenate(split_pair(own_ref[s], own_ref[s + 1]), axis=0))
        return pairs, results

    red_ref[...] = jnp.zeros_like(red_ref)

    def batch(b, carry):
        lax.fori_loop((b + 1) * BATCH, jnp.minimum(b + 2, last) * BATCH, start, 0)
        for j in range(BATCH):
            fetch(b * BATCH + j).wait()
        pairs, results = [], []
        for j in range(BATCH):
            x, y = product(b * BATCH + j)
            pairs += x
            results += y
        red_ref[...] += lax.dot_general(
            jnp.concatenate(pairs, axis=1),
            jnp.concatenate(results, axis=1),
            NT,
            precision=HIGH,
            preferred_element_type=jnp.float32,
        )
        return carry

    lax.fori_loop(first, last, batch, 0)


def fill_zero(xh_ref, xl_ref):
    xh_ref[xh_ref.shape[0] - 1] = jnp.zeros(xh_ref.shape[1:], jnp.bfloat16)
    xl_ref[xl_ref.shape[0] - 1] = jnp.zeros(xl_ref.shape[1:], jnp.bfloat16)


def near_kernel(order_ref, cols_ref, near_ref, own_ref, jac_hbm, out_ref, red_ref, xh_ref, xl_ref, jac_ref, sems):
    slots = own_ref.shape[0]
    odd = my_part() % 2

    def prepare():
        fill(near_ref, xh_ref, xl_ref, (1 - odd) * (slots + RIM))
        fill(own_ref, xh_ref, xl_ref, RIM)
        fill_zero(xh_ref, xl_ref)

    batches = order_ref[slots // GROUP]
    run_batches(0, batches, cols_ref, own_ref, jac_hbm, out_ref, red_ref, xh_ref, xl_ref, jac_ref, order_ref, sems, prepare)


def far_kernel(order_ref, cols_ref, far_ref, own_ref, done_ref, red_in_ref, th_ref, tl_ref, jac_hbm, out_ref, keep_ref, give_ref, red_ref, gram_ref, pairs_ref, table_sems, xh_ref, xl_ref, jac_ref, sems):
    slots = own_ref.shape[0]
    odd = my_part() % 2

    def prepare():
        copies = (
            pltpu.make_async_copy(th_ref, xh_ref, table_sems.at[0]),
            pltpu.make_async_copy(tl_ref, xl_ref, table_sems.at[1]),
            pltpu.make_async_copy(done_ref, out_ref, table_sems.at[2]),
        )
        for copy in copies:
            copy.start()
        make_pairs(own_ref, pairs_ref)
        pairs = pairs_ref[...]
        gram_ref[...] = lax.dot_general(pairs, pairs, NT, precision=HIGH, preferred_element_type=jnp.float32)
        for copy in copies:
            copy.wait()
        fill(far_ref, xh_ref, xl_ref, odd * (slots + RIM))

    batches = order_ref[slots // GROUP]
    last = slots // GROUP // BATCH
    run_batches(batches, last, cols_ref, own_ref, jac_hbm, out_ref, red_ref, xh_ref, xl_ref, jac_ref, order_ref, sems, prepare)

    gram = to_tile(gram_ref[...])
    reduced = to_tile(red_in_ref[...] + red_ref[...])
    keep_ref[...] = jnp.where(odd == 1, reduced, gram)
    give_ref[...] = jnp.where(odd == 1, gram, reduced)


def apply_near(order, cols, near, own, jac_split):
    slots = own.shape[0]
    table = jax.ShapeDtypeStruct((slots + 2 * RIM + 1, NSNAP, LANES), jnp.bfloat16)
    return pl.pallas_call(
        near_kernel,
        out_shape=(
            jax.ShapeDtypeStruct((slots, HALF, LANES), jnp.float32),
            jax.ShapeDtypeStruct((NSNAP, NSNAP), jnp.float32),
            table,
            table,
        ),
        in_specs=[spec(SMEM)] * 2 + [spec(VMEM)] * 2 + [spec(pl.ANY)],
        out_specs=(spec(VMEM),) * 4,
        scratch_shapes=[
            pltpu.VMEM(jac_split.shape, jac_split.dtype),
            pltpu.SemaphoreType.DMA((slots // GROUP,)),
        ],
        compiler_params=limit(46),
        cost_estimate=cost(2 * 3 * slots * 3 * NSNAP * 512 * BS, 20 * 1024 * 1024),
        name="apply_near",
    )(order, cols, near, own, jac_split)


def apply_far(order, cols, far, own, done, jac_split):
    slots = own.shape[0]
    tile = jax.ShapeDtypeStruct((8, LANES), jnp.float32)
    table = pltpu.VMEM(done[2].shape, done[2].dtype)
    return pl.pallas_call(
        far_kernel,
        out_shape=(jax.ShapeDtypeStruct((slots, HALF, LANES), jnp.float32), tile, tile),
        in_specs=[spec(SMEM)] * 2 + [spec(VMEM)] * 6 + [spec(pl.ANY)],
        out_specs=(spec(VMEM),) * 3,
        scratch_shapes=[
            pltpu.VMEM((NSNAP, NSNAP), jnp.float32),
            pltpu.VMEM((NSNAP, NSNAP), jnp.float32),
            pltpu.VMEM((NSNAP, slots * BS), jnp.float32),
            pltpu.SemaphoreType.DMA((3,)),
            table,
            table,
            pltpu.VMEM(jac_split.shape, jac_split.dtype),
            pltpu.SemaphoreType.DMA((slots // GROUP,)),
        ],
        compiler_params=limit(46),
        cost_estimate=cost(2 * 3 * slots * NSNAP * 512 * BS, 8 * 1024 * 1024),
        name="apply_far",
    )(order, cols, far, own, *done, jac_split)


def factor(gram, total_rows):
    groups = range(NSNAP // 8)
    row = lax.broadcasted_iota(jnp.int32, (8, LANES), 0)
    lane = lax.broadcasted_iota(jnp.int32, (8, LANES), 1)
    rank = [2 * ((row + 8 * v) % HALF) + (row + 8 * v) // HALF for v in groups]
    work = [
        jnp.where(lane < NSNAP, gram[v], jnp.where(lane - NSNAP == row + 8 * v, 1.0, 0.0).astype(jnp.float32))
        for v in groups
    ]
    row_of = lambda x, p: jnp.broadcast_to(x[p // 8][p % 8 : p % 8 + 1, :], (8, LANES))
    step = 8
    for first in range(0, NSNAP, step):
        at = [(k % 2) * HALF + k // 2 for k in range(first, first + step)]
        rows = [row_of(work, p) for p in at]
        cols = [[jnp.broadcast_to(x[:, p : p + 1], (8, LANES)) for x in work] for p in at]
        block = [[row_of(cols[n], at[m]) for n in range(step)] for m in range(step)]
        below = [jnp.zeros((8, LANES), jnp.float32) for _ in groups]
        for m in range(step):
            inverse = 1.0 / block[m][m]
            for v in groups:
                ratio = cols[m][v] * inverse
                below[v] = below[v] + ratio * rows[m]
                for n in range(m + 1, step):
                    cols[n][v] = cols[n][v] - ratio * block[m][n]
            for n in range(m + 1, step):
                ratio = block[n][m] * inverse
                rows[n] = rows[n] - ratio * rows[m]
                block[n] = [x - ratio * y for x, y in zip(block[n], block[m])]
        for v in groups:
            new = jnp.where(rank[v] >= first + step, work[v] - below[v], work[v])
            for m in range(step):
                if at[m] // 8 == v:
                    new = jnp.where(row == at[m] % 8, rows[m], new)
            work[v] = new
    scaled = []
    for v in groups:
        diag = jnp.sum(jnp.where(lane == row + 8 * v, work[v], 0.0), axis=1, keepdims=True)
        scaled.append(pltpu.roll(work[v], LANES - NSNAP, 1) * (float(total_rows) ** 0.5 / jnp.sqrt(diag)))
    return jnp.concatenate(scaled, axis=0)


def finish(scaled, reduced):
    row = lax.broadcasted_iota(jnp.int32, (NSNAP, NSNAP), 0)
    col = lax.broadcasted_iota(jnp.int32, (NSNAP, NSNAP), 1)
    place = jnp.where(col == (row % 2) * HALF + row // 2, 1.0, 0.0).astype(jnp.float32)
    dot = lambda a, b, dims: lax.dot_general(a, b, dims, precision=HIGH, preferred_element_type=jnp.float32)
    nn = (((1,), (0,)), ((), ()))
    natural = dot(place, scaled, nn)
    return dot(dot(natural, reduced, nn), natural, NT)


def mix_kernel(total_rows, sums_ref, snap_ref, jac_ref, basis_ref, out_ref, final_ref, same_ref, swap_ref, plain_ref, turned_ref):
    low = low_half((HALF, LANES))

    @pl.when(pl.program_id(0) == 0)
    def _():
        n_part = sums_ref.shape[0]
        gram = tree_sum([sums_ref[p] for p in range(0, n_part, 2)])
        scaled = factor(from_tile(gram), total_rows)
        reduced = tree_sum([sums_ref[p] for p in range(1, n_part, 2)])
        reduced = jnp.concatenate(from_tile(reduced), axis=0)[:, 0:NSNAP]
        final_ref[...] = finish(scaled[:, 0:NSNAP], reduced) / float(total_rows)
        wide = lambda kk, j: jnp.broadcast_to(scaled[kk * HALF : kk * HALF + HALF, j : j + 1], (HALF, LANES))
        for j2 in range(HALF):
            same_ref[j2] = jnp.where(low, wide(0, j2), wide(1, HALF + j2))
            swap_ref[j2] = jnp.where(low, wide(0, HALF + j2), wide(1, j2))

    both = range(2)
    for source, target in ((snap_ref, basis_ref), (jac_ref, out_ref)):
        def body(pair, carry):
            for j2 in range(HALF):
                for h in both:
                    x = source[pl.ds((2 * pair + h) * 8 * HALF + j2, 8, stride=HALF), :]
                    plain_ref[h, j2] = x
                    turned_ref[h, j2] = pltpu.roll(x, BS, 1)
            for k4 in range(0, HALF, 4):
                totals = {}
                for j2 in range(k4 + 4):
                    values = [(plain_ref[h, j2], turned_ref[h, j2]) for h in both]
                    for k2 in range(max(k4, j2), k4 + 4):
                        same = jnp.broadcast_to(same_ref[j2, k2 : k2 + 1, :], (8, LANES))
                        swap = jnp.broadcast_to(swap_ref[j2, k2 : k2 + 1, :], (8, LANES))
                        for h in both:
                            term = same * values[h][0] + swap * values[h][1]
                            totals[k2, h] = totals[k2, h] + term if j2 else term
                for k2 in range(k4, k4 + 4):
                    for h in both:
                        rows = pl.ds(pl.multiple_of((2 * pair + h) * 8, 8), 8)
                        target[rows, LANES * k2 : LANES * k2 + LANES] = totals[k2, h]
            return carry

        lax.fori_loop(0, target.shape[0] // 16, body, 0, unroll=2)


def mix(sums, snaps, jac, total_rows):
    slots = snaps.shape[0]
    step = 32
    out = jax.ShapeDtypeStruct((slots, NSNAP * BS), jnp.float32)
    flat = lambda x: x.reshape(slots * HALF, LANES)
    rows = pl.BlockSpec((step * HALF, LANES), lambda i: (i, 0))
    return pl.pallas_call(
        lambda *refs: mix_kernel(total_rows, *refs),
        out_shape=(out, out, jax.ShapeDtypeStruct((NSNAP, NSNAP), jnp.float32)),
        grid=(slots // step,),
        in_specs=[pl.BlockSpec(sums.shape, lambda i: (0, 0, 0)), rows, rows],
        out_specs=[pl.BlockSpec((step, NSNAP * BS), lambda i: (i, 0))] * 2 + [pl.BlockSpec((NSNAP, NSNAP), lambda i: (0, 0))],
        scratch_shapes=[pltpu.VMEM((HALF, HALF, LANES), jnp.float32)] * 2 + [pltpu.VMEM((2, HALF, 8, LANES), jnp.float32)] * 2,
        cost_estimate=cost(2 * 2 * slots * BS * NSNAP * NSNAP, 4 * 1024 * 1024),
        compiler_params=limit(12),
        name="mix",
    )(sums, flat(snaps), flat(jac))


def exchange(tiles):
    return lax.all_to_all(tiles, AXES, split_axis=0, concat_axis=0, tiled=True)


def shards(snapshots, part_map, jac_blocks, jac_cols):
    n_part = lax.axis_size("file") * lax.axis_size("rows")
    blocks = jac_blocks.shape[0]
    total_rows = blocks * BS * n_part

    cols = jac_cols.T
    packed, table = pack(snapshots, part_map, cols, n_part)
    received = exchange(packed)
    jac_split, order = split_blocks(jac_blocks, table)
    received, jac_split, order = lax.optimization_barrier((received, jac_split, order))
    snaps, near, far = assemble(received, table, blocks)

    near_swap = [(p, p ^ 1) for p in range(n_part)]
    far_swap = [(p, ((p + 1) ^ 1) - 1) for p in range(1, n_part - 1)]
    far = lax.ppermute(far, AXES, far_swap)
    near = lax.ppermute(near, AXES, near_swap)
    done = apply_near(order, cols, near, snaps, jac_split)
    done, far = lax.optimization_barrier((done, far))
    jac_snaps, keep, give = apply_far(order, cols, far, snaps, done, jac_split)
    pair_sum = keep + lax.ppermute(give, AXES, near_swap)
    sums = exchange(jnp.broadcast_to(pair_sum[None], (n_part, 8, LANES)))
    return mix(sums, snaps, jac_snaps, total_rows)


def solution(mesh):
    in_specs = (P("rows", "file"), P(), P(AXES, None, None), P(AXES, None))
    out_specs = (P(AXES, None), P(AXES, None), P())
    return jax.shard_map(shards, mesh=mesh, in_specs=in_specs, out_specs=out_specs, check_vma=False)
```
